32 devices in a mesh: near: 16 (over z, y, x), far: 2 (over core).
Axes of the slice: x: 2, y: 2, z: 4, core: 2. Of those that a mesh axis runs over, the one named last changes fastest.
Arguments:
- vectors: bfloat16 [128, 4, 480], P('near'), may hold values from -6 to 6
- near_blocks: bfloat16 [128, 16, 2, 240, 240], P('near', 'far'), may hold values from -0.09375 to 0.09375
- neighbours: int32 [128, 16], P('near', 'far'), may hold values from 0 to 127, as said below
- live_counts: int32 [128], P('near'), may hold values from 4 to 16, as said below
- tmatrix: float32 [128, 2, 240], P('near'), may hold values from -0.8 to 0.8
- agg_matrix: bfloat16 [480, 512], replicated, may hold values from -0.25 to 0.25
- sphere_box: int32 [128], P('near'), may hold values from 0 to 15, never falling along the last dimension, each value on 1 to 24 neighbouring positions
- agg_angle: float32 [128, 256], P('near'), may hold values from -3.140625 to 3.140625
- far_list: int32 [16, 16], P('far'), may hold values from 0 to 15, as said below
- far_factors: float32 [16, 16, 2, 256], P('far', None, None, 'near'), may hold values from -0.6 to 0.6
- dis_matrix: bfloat16 [512, 480], replicated, may hold values from -0.25 to 0.25
Outputs:
- first_image: bfloat16 [128, 4, 480], P('near')
- second_image: bfloat16 [128, 4, 480], P('near')
The draws below stay inside these ranges and needn't reach their ends.
Inputs may be any that keep to these rules, and one draw needn't show every extreme that they name: `neighbours`: each entry differs from its row's sphere number by 1 to 8. `live_counts`: slots at or above a sphere's count are padding; some sphere has all 16 slots live. `sphere_box`: box numbers never fall along the spheres; every box holds 1 to 24 spheres. `far_list`: a box's far list names neither the box nor the boxes numbered one above or below it, counted around.
All inputs are finite; a program needn't handle non-finite values.
Results may differ from the reference program's by a relative error of at most 0.0052.
Values may be sent and summed in bfloat16 or wider, within the bound.
No kernel may reach another device: no remote copies, remote signals or barrier semaphores. Data moves between devices by JAX's collectives and lax.ppermute only.
A program may use at most 64 MiB of HBM per device.

```python
import math
import jax
import jax.numpy as jnp
import numpy as np
from jax import lax

C = 240
Q = 256
R = 4
K = 16
FL = 16
SPH_DEV = 8
SPHERES = 128
BOXES = 16
MOST_BOX = 24


def draw_neighbours(key, part):
    first_key, second_key = jax.random.split(key)
    offsets = jax.random.randint(first_key, (SPHERES, K), 1, SPH_DEV + 1)
    signs = jax.random.randint(second_key, (SPHERES, K), 0, 2) * 2 - 1
    anchor = jnp.arange(SPHERES, dtype=jnp.int32)[:, None]
    target = anchor + signs * offsets
    inside = (target >= 0) & (target < SPHERES)
    return jnp.where(inside, target, anchor - signs * offsets).astype(jnp.int32)


def draw_live_counts(key, part):
    counts = jax.random.randint(key, (SPHERES,), K // 4, K + 1)
    return counts.at[0].set(K).astype(jnp.int32)


def draw_far_list(key, part):
    anchor = jnp.arange(BOXES, dtype=jnp.int32)[:, None]
    offsets = jax.random.randint(key, (BOXES, FL), 2, BOXES - 1)
    return ((anchor + offsets) % BOXES).astype(jnp.int32)


def levels(rng, extent, cuts, low, largest):
    level = 1.0
    for position, blocks in cuts:
        draws = jax.random.uniform(jax.random.fold_in(jax.random.fold_in(rng, 6), position), (blocks,), jnp.float32, low / len(cuts), largest / len(cuts))
        level = level * jnp.repeat(jnp.exp(draws), extent[position] // blocks).reshape((-1,) + (1,) * (len(extent) - 1 - position))
    return level


def length_profile(amount, total, limit, slope):
    loads = [(1 << 20) // math.isqrt(rank ** slope) + 1 for rank in range(2, amount + 1)]
    rest, given = total - limit - (amount - 1), [1] * (amount - 1)
    while rest > 0:
        free = [i for i in range(amount - 1) if given[i] < limit]
        whole, budget = sum([loads[i] for i in free]), rest
        for i in free:
            extra = min(limit - given[i], max(1, budget * loads[i] // whole), rest)
            given[i] = given[i] + extra
            rest = rest - extra
    return np.array([limit] + given)


def uneven(key, count, total, most, lean):
    if count == 2:
        one = jax.random.randint(key, (), max(1, total - most), min(most, total - 1) + 1)
        return jnp.stack([one, total - one])
    sizes = jnp.asarray(length_profile(count, total, most, lean), jnp.int32)
    twos = (count - 1) // 2
    source_of, receiver = sizes[1:1 + 2 * twos:2], sizes[2:2 + 2 * twos:2]
    margin = jnp.minimum(source_of - 1, most - receiver)
    passed = jax.random.randint(jax.random.fold_in(key, 1), (twos,), 0, 1 << 20) % (margin + 1)
    sizes = sizes.at[1:1 + 2 * twos:2].set(source_of - passed).at[2:2 + 2 * twos:2].set(receiver + passed)
    return sizes[jax.random.permutation(jax.random.fold_in(key, 2), count)]


def noise(stream_key, dims, scale, most, shards=(), kind=jnp.bfloat16):
    entries = scale * jax.random.normal(stream_key, dims, jnp.float32)
    if shards:
        entries = entries * levels(stream_key, dims, shards, -0.22, 0.18)
    return jnp.clip(entries, -most, most).astype(kind)


def setup_inputs(seed: int = 0) -> dict:
    arg_keys = jax.random.split(jax.random.key(seed), 12)
    vectors = noise(arg_keys[0], (SPHERES, R, 2 * C), 1.0, 6.0, ((0, 16),))
    near_blocks = noise(arg_keys[1], (SPHERES, K, 2, C, C), (C * K) ** -0.5, 0.09375, ((0, 16), (1, 2)))
    neighbours = draw_neighbours(jax.random.fold_in(arg_keys[11], 71), 0)
    live_counts = draw_live_counts(jax.random.fold_in(arg_keys[11], 71), 0)
    tmatrix = jnp.clip(jax.random.uniform(arg_keys[4], (SPHERES, 2, C), jnp.float32, -0.8, 0.8) * levels(arg_keys[4], (SPHERES, 2, C), ((0, 16),), -0.4, 0.0), -0.8, 0.8)
    agg_matrix = noise(arg_keys[5], (2 * C, 2 * Q), (2 * C) ** -0.5, 0.25)
    sphere_box = jnp.searchsorted(jnp.cumsum(uneven(arg_keys[6], BOXES, SPHERES, MOST_BOX, 2)), jnp.arange(SPHERES), side="right").astype(jnp.int32)
    agg_angle = jnp.clip(jax.random.uniform(arg_keys[7], (SPHERES, Q), jnp.float32, -3.140625, 3.140625), -3.140625, 3.140625)
    far_list = draw_far_list(jax.random.fold_in(arg_keys[11], 71), 0)
    far_factors = noise(arg_keys[9], (BOXES, FL, 2, Q), 0.1, 0.6, ((0, 2), (3, 16)), jnp.float32)
    dis_matrix = noise(arg_keys[10], (2 * Q, 2 * C), (2 * Q) ** -0.5, 0.25)
    return dict(vectors=vectors, near_blocks=near_blocks, neighbours=neighbours, live_counts=live_counts, tmatrix=tmatrix, agg_matrix=agg_matrix, sphere_box=sphere_box, agg_angle=agg_angle, far_list=far_list, far_factors=far_factors, dis_matrix=dis_matrix)


def complex_mul(left_re, left_im, right_re, right_im):
    return left_re * right_re - left_im * right_im, left_re * right_im + left_im * right_re


def realify(block):
    real_part = block[..., 0, :, :]
    imag_part = block[..., 1, :, :]
    upper = jnp.concatenate([real_part, imag_part], axis=-1)
    lower = jnp.concatenate([-imag_part, real_part], axis=-1)
    return jnp.concatenate([upper, lower], axis=-2)


def apply_operator(current, near_blocks, neighbours, live_counts, tmatrix, agg_matrix, sphere_box, agg_angle, far_list, far_factors, dis_matrix):
    spheres, newton, width = current.shape
    coeffs = width // 2
    slots = neighbours.shape[1]
    boxes = far_list.shape[0]
    waves = agg_matrix.shape[1] // 2

    def near_one(packed):
        blocks, sources, count = packed
        gathered = current[sources].astype(jnp.float32)
        alive = (jnp.arange(slots) < count).astype(jnp.float32)
        gathered = gathered * alive[:, None, None]
        matrix = realify(blocks).astype(jnp.float32)
        return jnp.einsum("krc,kcd->rd", gathered, matrix, precision=lax.Precision.HIGHEST)

    near_field = lax.map(near_one, (near_blocks, neighbours, live_counts))
    cosine = jnp.cos(agg_angle)[:, None, :]
    sine = jnp.sin(agg_angle)[:, None, :]
    outgoing = jnp.dot(current.reshape(spheres * newton, width), agg_matrix, preferred_element_type=jnp.float32)
    outgoing = outgoing.reshape(spheres, newton, 2, waves)
    out_re, out_im = complex_mul(outgoing[:, :, 0], outgoing[:, :, 1], cosine, sine)
    stacked = jnp.stack([out_re, out_im], axis=2)
    box_waves = jax.ops.segment_sum(stacked, sphere_box, num_segments=boxes)
    picked = box_waves[far_list]
    in_re, in_im = complex_mul(far_factors[:, :, None, 0, :], far_factors[:, :, None, 1, :], picked[:, :, :, 0], picked[:, :, :, 1])
    incoming_re = jnp.sum(in_re, axis=1)
    incoming_im = jnp.sum(in_im, axis=1)
    sphere_re = incoming_re[sphere_box]
    sphere_im = incoming_im[sphere_box]
    local_re, local_im = complex_mul(sphere_re, sphere_im, cosine, -sine)
    local_waves = jnp.concatenate([local_re, local_im], axis=-1).astype(jnp.bfloat16)
    far_field = jnp.dot(local_waves.reshape(spheres * newton, 2 * waves), dis_matrix, preferred_element_type=jnp.float32)
    field = near_field + far_field.reshape(spheres, newton, width)
    scat_re, scat_im = complex_mul(tmatrix[:, None, 0, :], tmatrix[:, None, 1, :], field[..., :coeffs], field[..., coeffs:])
    image = current.astype(jnp.float32) - jnp.concatenate([scat_re, scat_im], axis=-1)
    return image.astype(jnp.bfloat16)


def reference(vectors, near_blocks, neighbours, live_counts, tmatrix, agg_matrix, sphere_box, agg_angle, far_list, far_factors, dis_matrix):
    first_image = apply_operator(vectors, near_blocks, neighbours, live_counts, tmatrix, agg_matrix, sphere_box, agg_angle, far_list, far_factors, dis_matrix)
    second_image = apply_operator(first_image, near_blocks, neighbours, live_counts, tmatrix, agg_matrix, sphere_box, agg_angle, far_list, far_factors, dis_matrix)
    return first_image, second_image
```

```python
import jax
import jax.numpy as jnp
from jax import lax
from jax.sharding import PartitionSpec as P

F32 = jnp.float32
BF16 = jnp.bfloat16
RADIX = 4


def complex_mul(left_re, left_im, right_re, right_im):
    return (left_re * right_re - left_im * right_im, left_re * right_im + left_im * right_re)


def swap_near(block, mask):
    count = lax.axis_size("near")
    return lax.ppermute(block, "near", [(i, i ^ mask) for i in range(count)])


def phase_masks():
    count = lax.axis_size("near")
    phases, step = [], 1
    while step < count:
        radix = min(RADIX, count // step)
        phases.append([step * j for j in range(1, radix)])
        step *= radix
    return phases


def xor_gather(block, masks):
    return [block] + [swap_near(block, mask) for mask in masks]


def in_order(parts, masks):
    step = masks[0]
    digit = lax.axis_index("near") // step % len(parts)
    stacked = jnp.stack(parts)
    return jnp.take(stacked, jnp.arange(len(parts)) ^ digit, axis=0)


def edge_rows(block):
    count = lax.axis_size("near")
    pairs = []
    for low in range(RADIX, count, RADIX):
        pairs.append((low - 1, low))
        pairs.append((low, low - 1))
    return lax.ppermute(block, "near", pairs) if pairs else jnp.zeros_like(block)


def over_far(block):
    count = lax.axis_size("far")
    if count == 2:
        other = lax.ppermute(block, "far", [(0, 1), (1, 0)])
        first = lax.axis_index("far") == 0
        return jnp.stack([jnp.where(first, block, other), jnp.where(first, other, block)])
    return lax.all_gather(block, "far", axis=0)


def near_share(partial, share):
    count = lax.axis_size("far")
    far_pos = lax.axis_index("far")
    mine = lax.dynamic_slice_in_dim(partial, far_pos % (partial.shape[1] // share) * share, share, 1)
    if count == 2:
        theirs = lax.dynamic_slice_in_dim(partial, (1 - far_pos) * share, share, 1)
        return mine + lax.ppermute(theirs, "far", [(0, 1), (1, 0)])
    total = lax.psum(partial, "far")
    return lax.dynamic_slice_in_dim(total, far_pos % (partial.shape[1] // share) * share, share, 1)


def shards(
    vectors,
    near_blocks,
    neighbours,
    live_counts,
    tmatrix,
    agg_matrix,
    sphere_box,
    agg_angle,
    far_list,
    far_factors,
    dis_matrix,
):
    spheres, newton, width = vectors.shape
    coeffs = width // 2
    slots = neighbours.shape[1]
    far_count = lax.axis_size("far")
    near_count = lax.axis_size("near")
    own_boxes, listed = far_list.shape
    boxes = own_boxes * far_count
    waves = agg_matrix.shape[1] // 2
    share = newton // min(far_count, newton)
    splits = newton // share
    near_pos = lax.axis_index("near")
    far_pos = lax.axis_index("far")
    phases = phase_masks()
    rows = spheres * share

    def own_share(block):
        return lax.dynamic_slice_in_dim(block, far_pos % splits * share, share, 1)

    hi = agg_angle.astype(BF16)
    low = (agg_angle - hi.astype(F32)).astype(BF16)
    factors = far_factors.astype(BF16).reshape(-1, far_factors.shape[-1]).T
    per_part = factors.size
    lists = over_far_lists(far_list)
    extra = jnp.concatenate(
        [
            jnp.repeat(sphere_box, share).astype(BF16)[:, None],
            jnp.stack([hi, low]).reshape(rows, -1),
            factors.reshape(rows, -1),
        ],
        axis=1,
    )
    angle_width = 2 * spheres * waves // rows

    cosine = jnp.cos(agg_angle)
    sine = jnp.sin(agg_angle)
    alive = (far_pos * slots + jnp.arange(slots, dtype=jnp.int32))[None, :] < live_counts[:, None]
    chip = neighbours // spheres
    place = jnp.where(chip // RADIX == near_pos // RADIX, chip ^ near_pos, RADIX)
    local_index = place * spheres + neighbours % spheres

    state = {}
    images = []
    current = own_share(vectors)
    whole = vectors
    for step in range(2):
        flat = current.reshape(rows, width)
        edge = edge_rows(current)
        message = jnp.concatenate([flat, extra], axis=1) if step == 0 else flat
        parts = xor_gather(message, phases[0])
        group = len(parts)
        around = [p[:, :width].reshape(spheres, share, width) for p in parts]
        full = over_far(jnp.stack(around + [edge]))[:splits]
        full = jnp.moveaxis(full, 0, 2).reshape((group + 1) * spheres, newton, width)
        if step == 1:
            images.append(full[:spheres])
        if step == 0:
            box_ids = jnp.concatenate([p[:, width].reshape(spheres, share)[:, 0] for p in parts])
            angles = jnp.stack(
                [
                    p[:, width + 1 : width + 1 + angle_width].reshape(2, spheres, waves)
                    for p in parts
                ]
            ).astype(F32)
            angles = (angles[:, 0] + angles[:, 1]).reshape(group * spheres, waves)
            state["cos"], state["sin"] = jnp.cos(angles), jnp.sin(angles)
            state["member"] = (
                box_ids.astype(jnp.int32)[None, :] == jnp.arange(boxes, dtype=jnp.int32)[:, None]
            ).astype(F32)
            table = in_order([p[:, width + 1 + angle_width :] for p in parts], phases[0])
        product = jnp.dot(
            jnp.concatenate(around).reshape(group * rows, width),
            agg_matrix,
            preferred_element_type=F32,
        ).reshape(group * spheres, share, 2, waves)
        out_re, out_im = complex_mul(
            product[:, :, 0], product[:, :, 1], state["cos"][:, None], state["sin"][:, None]
        )
        stacked = jnp.concatenate([out_re, out_im], axis=-1)
        sums = jnp.einsum("bn,nrq->brq", state["member"], stacked, precision=lax.Precision.HIGHEST)
        for masks in phases[1:]:
            block = sums.astype(BF16).reshape(boxes * share, 2 * waves)
            if step == 0:
                block = jnp.concatenate([block, table.reshape(boxes * share, -1)], axis=1)
            pieces = xor_gather(block, masks)
            sums = sum(p[:, : 2 * waves].astype(F32) for p in pieces)
            sums = sums.reshape(boxes, share, 2 * waves)
            if step == 0:
                table = in_order([p[:, 2 * waves :] for p in pieces], masks)
        if step == 0:
            table = over_far(table.reshape(waves, own_boxes, listed, 2))
            table = table.transpose(0, 2, 3, 4, 1).reshape(boxes, listed, 2, waves)
            state["factors"] = table[sphere_box].astype(F32)
            state["sources"] = (
                lists[sphere_box][:, :, None] == jnp.arange(boxes, dtype=jnp.int32)
            ).astype(F32)
        gathered = jnp.where(alive[:, :, None, None], full[local_index], jnp.zeros((), BF16))
        both = jnp.concatenate([gathered[..., :coeffs], gathered[..., coeffs:]], axis=2)
        with_real = jnp.einsum(
            "nkrc,nkcd->nrd", both, near_blocks[:, :, 0], preferred_element_type=F32
        )
        with_imag = jnp.einsum(
            "nkrc,nkcd->nrd", both, near_blocks[:, :, 1], preferred_element_type=F32
        )
        near_re = with_real[:, :newton] - with_imag[:, newton:]
        near_im = with_imag[:, :newton] + with_real[:, newton:]
        near_field = near_share(jnp.concatenate([near_re, near_im], axis=-1), share)
        picked = jnp.einsum(
            "nfb,brq->nfrq", state["sources"], sums, precision=lax.Precision.HIGHEST
        )
        fac = state["factors"]
        in_re, in_im = complex_mul(
            fac[:, :, None, 0], fac[:, :, None, 1], picked[..., :waves], picked[..., waves:]
        )
        in_re, in_im = jnp.sum(in_re, axis=1), jnp.sum(in_im, axis=1)
        local_re, local_im = complex_mul(in_re, in_im, cosine[:, None], -sine[:, None])
        local_waves = jnp.concatenate([local_re, local_im], axis=-1).astype(BF16)
        far_field = jnp.dot(
            local_waves.reshape(rows, 2 * waves), dis_matrix, preferred_element_type=F32
        ).reshape(spheres, share, width)
        field = near_field + far_field
        scat_re, scat_im = complex_mul(
            tmatrix[:, None, 0], tmatrix[:, None, 1], field[..., :coeffs], field[..., coeffs:]
        )
        current = (current.astype(F32) - jnp.concatenate([scat_re, scat_im], axis=-1)).astype(BF16)
    last = over_far(current)[:splits]
    images.append(jnp.moveaxis(last, 0, 1).reshape(spheres, newton, width))
    return tuple(images)


def over_far_lists(far_list):
    gathered = over_far(far_list)
    return gathered.reshape(-1, far_list.shape[1])


def solution(mesh):
    return jax.shard_map(
        shards,
        mesh=mesh,
        in_specs=(
            P("near", None, None),
            P("near", "far", None, None, None),
            P("near", "far"),
            P("near"),
            P("near", None, None),
            P(),
            P("near"),
            P("near", None),
            P("far", None),
            P("far", None, None, "near"),
            P(),
        ),
        out_specs=(P("near", None, None), P("near", None, None)),
        check_vma=False,
    )
```

```python
import functools

import jax
import jax.numpy as jnp
from jax import lax
from jax.experimental import pallas as pl
from jax.experimental.pallas import tpu as pltpu
from jax.sharding import PartitionSpec as P

F32 = jnp.float32
BF16 = jnp.bfloat16
RADIX = 4


def complex_mul(left_re, left_im, right_re, right_im):
    return (left_re * right_re - left_im * right_im, left_re * right_im + left_im * right_re)


def swap_near(block, mask):
    count = lax.axis_size("near")
    return lax.ppermute(block, "near", [(i, i ^ mask) for i in range(count)])


def phase_masks():
    count = lax.axis_size("near")
    phases, step = [], 1
    while step < count:
        radix = min(RADIX, count // step)
        phases.append([step * j for j in range(1, radix)])
        step *= radix
    return phases


def xor_gather(block, masks):
    return [block] + [swap_near(block, mask) for mask in masks]


def in_order(parts, masks):
    step = masks[0]
    digit = lax.axis_index("near") // step % len(parts)
    stacked = jnp.stack(parts)
    return jnp.take(stacked, jnp.arange(len(parts)) ^ digit, axis=0)


def edge_rows(block):
    count = lax.axis_size("near")
    pairs = []
    for low in range(RADIX, count, RADIX):
        pairs.append((low - 1, low))
        pairs.append((low, low - 1))
    return lax.ppermute(block, "near", pairs) if pairs else jnp.zeros_like(block)


def over_far(block):
    count = lax.axis_size("far")
    if count == 2:
        other = lax.ppermute(block, "far", [(0, 1), (1, 0)])
        first = lax.axis_index("far") == 0
        return jnp.stack([jnp.where(first, block, other), jnp.where(first, other, block)])
    return lax.all_gather(block, "far", axis=0)


def near_share(partial, share):
    count = lax.axis_size("far")
    far_pos = lax.axis_index("far")
    mine = lax.dynamic_slice_in_dim(partial, far_pos % (partial.shape[1] // share) * share, share, 1)
    if count == 2:
        theirs = lax.dynamic_slice_in_dim(partial, (1 - far_pos) * share, share, 1)
        return mine + lax.ppermute(theirs, "far", [(0, 1), (1, 0)])
    total = lax.psum(partial, "far")
    return lax.dynamic_slice_in_dim(total, far_pos % (partial.shape[1] // share) * share, share, 1)


def plain_shards(
    vectors,
    near_blocks,
    neighbours,
    live_counts,
    tmatrix,
    agg_matrix,
    sphere_box,
    agg_angle,
    far_list,
    far_factors,
    dis_matrix,
):
    spheres, newton, width = vectors.shape
    coeffs = width // 2
    slots = neighbours.shape[1]
    far_count = lax.axis_size("far")
    near_count = lax.axis_size("near")
    own_boxes, listed = far_list.shape
    boxes = own_boxes * far_count
    waves = agg_matrix.shape[1] // 2
    share = newton // min(far_count, newton)
    splits = newton // share
    near_pos = lax.axis_index("near")
    far_pos = lax.axis_index("far")
    phases = phase_masks()
    rows = spheres * share

    def own_share(block):
        return lax.dynamic_slice_in_dim(block, far_pos % splits * share, share, 1)

    rounded = lax.reduce_precision(agg_angle, 8, 7)
    hi, low = rounded.astype(BF16), (agg_angle - rounded).astype(BF16)
    factors = far_factors.astype(BF16).reshape(-1, far_factors.shape[-1]).T
    per_part = factors.size
    lists = over_far_lists(far_list)
    extra = jnp.concatenate(
        [
            jnp.repeat(sphere_box, share).astype(BF16)[:, None],
            jnp.stack([hi, low]).reshape(rows, -1),
            factors.reshape(rows, -1),
        ],
        axis=1,
    )
    angle_width = 2 * spheres * waves // rows

    cosine = jnp.cos(agg_angle)
    sine = jnp.sin(agg_angle)
    alive = (far_pos * slots + jnp.arange(slots, dtype=jnp.int32))[None, :] < live_counts[:, None]
    chip = neighbours // spheres
    place = jnp.where(chip // RADIX == near_pos // RADIX, chip ^ near_pos, RADIX)
    local_index = place * spheres + neighbours % spheres

    state = {}
    images = []
    current = own_share(vectors)
    whole = vectors
    for step in range(2):
        flat = current.reshape(rows, width)
        edge = edge_rows(current)
        message = jnp.concatenate([flat, extra], axis=1) if step == 0 else flat
        parts = xor_gather(message, phases[0])
        group = len(parts)
        around = [p[:, :width].reshape(spheres, share, width) for p in parts]
        full = over_far(jnp.stack(around + [edge]))[:splits]
        full = jnp.moveaxis(full, 0, 2).reshape((group + 1) * spheres, newton, width)
        if step == 1:
            images.append(full[:spheres])
        if step == 0:
            box_ids = jnp.concatenate([p[:, width].reshape(spheres, share)[:, 0] for p in parts])
            angles = jnp.stack(
                [
                    p[:, width + 1 : width + 1 + angle_width].reshape(2, spheres, waves)
                    for p in parts
                ]
            ).astype(F32)
            angles = (angles[:, 0] + angles[:, 1]).reshape(group * spheres, waves)
            state["cos"], state["sin"] = jnp.cos(angles), jnp.sin(angles)
            state["member"] = (
                box_ids.astype(jnp.int32)[None, :] == jnp.arange(boxes, dtype=jnp.int32)[:, None]
            ).astype(F32)
            table = in_order([p[:, width + 1 + angle_width :] for p in parts], phases[0])
        product = jnp.dot(
            jnp.concatenate(around).reshape(group * rows, width),
            agg_matrix,
            preferred_element_type=F32,
        ).reshape(group * spheres, share, 2, waves)
        out_re, out_im = complex_mul(
            product[:, :, 0], product[:, :, 1], state["cos"][:, None], state["sin"][:, None]
        )
        stacked = jnp.concatenate([out_re, out_im], axis=-1)
        sums = jnp.einsum("bn,nrq->brq", state["member"], stacked, precision=lax.Precision.HIGHEST)
        for masks in phases[1:]:
            block = sums.astype(BF16).reshape(boxes * share, 2 * waves)
            if step == 0:
                block = jnp.concatenate([block, table.reshape(boxes * share, -1)], axis=1)
            pieces = xor_gather(block, masks)
            sums = sum(p[:, : 2 * waves].astype(F32) for p in pieces)
            sums = sums.reshape(boxes, share, 2 * waves)
            if step == 0:
                table = in_order([p[:, 2 * waves :] for p in pieces], masks)
        if step == 0:
            table = over_far(table.reshape(waves, own_boxes, listed, 2))
            table = table.transpose(0, 2, 3, 4, 1).reshape(boxes, listed, 2, waves)
            state["factors"] = table[sphere_box].astype(F32)
            state["sources"] = (
                lists[sphere_box][:, :, None] == jnp.arange(boxes, dtype=jnp.int32)
            ).astype(F32)
        gathered = jnp.where(alive[:, :, None, None], full[local_index], jnp.zeros((), BF16))
        both = jnp.concatenate([gathered[..., :coeffs], gathered[..., coeffs:]], axis=2)
        with_real = jnp.einsum(
            "nkrc,nkcd->nrd", both, near_blocks[:, :, 0], preferred_element_type=F32
        )
        with_imag = jnp.einsum(
            "nkrc,nkcd->nrd", both, near_blocks[:, :, 1], preferred_element_type=F32
        )
        near_re = with_real[:, :newton] - with_imag[:, newton:]
        near_im = with_imag[:, :newton] + with_real[:, newton:]
        near_field = near_share(jnp.concatenate([near_re, near_im], axis=-1), share)
        picked = jnp.einsum(
            "nfb,brq->nfrq", state["sources"], sums, precision=lax.Precision.HIGHEST
        )
        fac = state["factors"]
        in_re, in_im = complex_mul(
            fac[:, :, None, 0], fac[:, :, None, 1], picked[..., :waves], picked[..., waves:]
        )
        in_re, in_im = jnp.sum(in_re, axis=1), jnp.sum(in_im, axis=1)
        local_re, local_im = complex_mul(in_re, in_im, cosine[:, None], -sine[:, None])
        local_waves = jnp.concatenate([local_re, local_im], axis=-1).astype(BF16)
        far_field = jnp.dot(
            local_waves.reshape(rows, 2 * waves), dis_matrix, preferred_element_type=F32
        ).reshape(spheres, share, width)
        field = near_field + far_field
        scat_re, scat_im = complex_mul(
            tmatrix[:, None, 0], tmatrix[:, None, 1], field[..., :coeffs], field[..., coeffs:]
        )
        current = (current.astype(F32) - jnp.concatenate([scat_re, scat_im], axis=-1)).astype(BF16)
    last = over_far(current)[:splits]
    images.append(jnp.moveaxis(last, 0, 1).reshape(spheres, newton, width))
    return tuple(images)


def over_far_lists(far_list):
    gathered = over_far(far_list)
    return gathered.reshape(-1, far_list.shape[1])


VM = pl.BlockSpec(memory_space=pltpu.VMEM)
SM = pl.BlockSpec(memory_space=pltpu.SMEM)


def call(kernel, outs, specs, args, scratch=(), flops=0, moved=0):
    return pl.pallas_call(
        kernel,
        out_shape=tuple(jax.ShapeDtypeStruct(shape, kind) for shape, kind in outs),
        in_specs=list(specs),
        out_specs=(VM,) * len(outs),
        scratch_shapes=list(scratch),
        cost_estimate=pl.CostEstimate(flops=flops, bytes_accessed=moved, transcendentals=0),
    )(*args)


def pack_kernel(place, box, vectors, angle, factors, out):
    spheres, newton, width = vectors.shape
    share = newton // 2
    waves = angle.shape[1]
    first = place[0] == 0
    values = vectors[...].astype(F32)
    for r in range(share):
        low, high = values[:, r], values[:, share + r]
        rows = pl.ds(r * spheres, spheres)
        out[rows, pl.ds(0, width)] = jnp.where(first, low, high).astype(BF16)
        out[rows, pl.ds(512, width)] = jnp.where(first, high, low).astype(BF16)
    lane = lax.broadcasted_iota(jnp.int32, (spheres * share, 512 - width), 0) % spheres
    ids = jnp.zeros((spheres * share, 512 - width), F32)
    for n in range(spheres):
        ids = jnp.where(lane == n, box[n].astype(F32), ids)
    out[:, pl.ds(width, 512 - width)] = ids.astype(BF16)
    hi = angle[...].astype(BF16)
    low = (angle[...] - hi.astype(F32)).astype(BF16)
    out[pl.ds(0, spheres), pl.ds(1024, waves)] = hi
    out[pl.ds(spheres, spheres), pl.ds(1024, waves)] = low
    out[:, pl.ds(1024 + waves, factors.shape[0])] = factors[...].T.astype(BF16)


def sum_rows(member, waves):
    dims = (((0,), (0,)), ((), ()))
    hi = waves.astype(BF16)
    low = (waves - hi.astype(F32)).astype(BF16)
    return lax.dot_general(member, hi, dims, preferred_element_type=F32) + lax.dot_general(
        member, low, dims, preferred_element_type=F32
    )


def turned(product, turn, waves):
    cosine, sine = turn[:, :waves], turn[:, waves:]
    re, im = product[:, :waves], product[:, waves:]
    return jnp.concatenate([re * cosine - im * sine, re * sine + im * cosine], axis=1)


def first_waves_kernel(boxes, place, p0, p1, p2, p3, agg, out, turn, member, table):
    parts = (p0, p1, p2, p3)
    width = agg.shape[0]
    waves = agg.shape[1] // 2
    rows = p0.shape[0]
    half = rows // 2
    held = table.shape[0] // 4
    for j, part in enumerate(parts):
        angle = part[pl.ds(0, half), pl.ds(1024, waves)].astype(F32)
        angle += part[pl.ds(half, half), pl.ds(1024, waves)].astype(F32)
        both = jnp.concatenate([jnp.cos(angle), jnp.sin(angle)], axis=1)
        turn[pl.ds(j * rows, half), :] = both
        turn[pl.ds(j * rows + half, half), :] = both
        ids = part[:, pl.ds(width, 1)].astype(F32)
        row = lax.broadcasted_iota(jnp.int32, (rows, 2 * boxes), 0) // half
        col = lax.broadcasted_iota(jnp.int32, (rows, 2 * boxes), 1)
        hit = (ids == (col % boxes).astype(F32)) & (row == col // boxes)
        member[pl.ds(j * rows, rows), :] = jnp.where(hit, 1.0, 0.0).astype(BF16)
        at = pl.multiple_of((place[1] ^ j) * held, held)
        table[pl.ds(at, held), :] = part[:, pl.ds(1024 + waves, table.shape[1])].astype(F32)
    flat = jnp.concatenate([p[:, pl.ds(0, width)] for p in parts], axis=0)
    product = jnp.dot(flat, agg[...], preferred_element_type=F32)
    sums = sum_rows(member[...], turned(product, turn[...], waves))
    out[:, pl.ds(0, 2 * waves)] = sums.astype(BF16)
    lines = out.shape[0]
    span = table.shape[1]
    for j in range(table.shape[0] // lines):
        out[:, pl.ds(2 * waves + j * span, span)] = table[pl.ds(j * lines, lines), :].astype(BF16)


def next_waves_kernel(p0, p1, p2, p3, agg, turn, member, out):
    waves = agg.shape[1] // 2
    flat = jnp.concatenate([p0[...], p1[...], p2[...], p3[...]], axis=0)
    product = jnp.dot(flat, agg[...], preferred_element_type=F32)
    out[...] = sum_rows(member[...], turned(product, turn[...], waves)).astype(BF16)


def table_kernel(waves, place, z0, z1, z2, z3, out, held):
    lines = z0.shape[0]
    span = held.shape[1]
    pieces = (z0.shape[1] - 2 * waves) // span
    for j, part in enumerate((z0, z1, z2, z3)):
        for i in range(pieces):
            at = pl.multiple_of(((place[2] ^ j) * pieces + i) * lines, lines)
            held[pl.ds(at, lines), :] = part[:, pl.ds(2 * waves + i * span, span)].astype(F32)
    out[...] = held[...].T.astype(BF16)


def near_kernel(starts, emit, place, neighbours, live, *refs):
    mine, theirs = refs[:5], refs[5 : 5 + (5 if starts[1] is not None else 1)]
    refs = refs[5 + len(theirs) :]
    blocks = refs[0]
    out_mine, out_theirs = refs[1], refs[2]
    image = refs[3] if emit else None
    held = refs[-1]
    n = pl.program_id(0)
    spheres = out_mine.shape[0] // 2
    slots = blocks.shape[1]
    coeffs = blocks.shape[3]

    @pl.when(n == 0)
    def _():
        for j in range(5):
            for side in range(2):
                for r in range(2):
                    rows = pl.ds(r * spheres, spheres)
                    if side == 0:
                        value = mine[j][rows, pl.ds(0, 2 * coeffs)]
                    elif starts[1] is not None:
                        value = theirs[j][rows, pl.ds(starts[1], 2 * coeffs)]
                    else:
                        value = theirs[0][pl.ds((2 * j + r) * spheres, spheres), :]
                    value = value.astype(F32)
                    at = pl.ds(j * spheres, spheres)
                    held[at, side * 2 + r, :] = value[:, :coeffs]
                    held[at, 4 + side * 2 + r, :] = value[:, coeffs:]
        if emit:
            first = place[0] == 0
            for r in range(2):
                own = mine[0][pl.ds(r * spheres, spheres), :].astype(F32)
                other = theirs[0][pl.ds(r * spheres, spheres), :].astype(F32)
                image[:, r, :] = jnp.where(first, own, other).astype(BF16)
                image[:, 2 + r, :] = jnp.where(first, other, own).astype(BF16)

    real = jnp.zeros((8, coeffs), F32)
    imag = jnp.zeros((8, coeffs), F32)
    for k in range(slots):
        source = neighbours[n, k]
        chip = source // spheres
        near = jnp.where(chip // 4 == place[3] // 4, chip ^ place[3], 4)
        value = held[near * spheres + source % spheres]
        alive = place[0] * slots + k < live[n]
        value = jnp.where(alive, value, 0.0).astype(BF16)
        real += jnp.dot(value, blocks[0, k, 0], preferred_element_type=F32)
        imag += jnp.dot(value, blocks[0, k, 1], preferred_element_type=F32)
    near_re = real[:4] - imag[4:]
    near_im = imag[:4] + real[4:]
    for r in range(2):
        row = pl.ds(r * spheres + n, 1)
        out_mine[row, pl.ds(0, coeffs)] = near_re[r : r + 1]
        out_mine[row, pl.ds(coeffs, coeffs)] = near_im[r : r + 1]
        out_theirs[row, pl.ds(0, coeffs)] = near_re[2 + r : 3 + r]
        out_theirs[row, pl.ds(coeffs, coeffs)] = near_im[2 + r : 3 + r]


def near_call(starts, emit, place, neighbours, live, mine, theirs, blocks):
    spheres, slots, _, coeffs, _ = blocks.shape
    rows = 2 * spheres
    outs = [jax.ShapeDtypeStruct((rows, 2 * coeffs), F32)] * 2
    if emit:
        outs.append(jax.ShapeDtypeStruct((spheres, 4, 2 * coeffs), BF16))
    full = [VM] * (len(mine) + len(theirs))
    return pl.pallas_call(
        functools.partial(near_kernel, starts, emit),
        grid=(spheres,),
        out_shape=tuple(outs),
        in_specs=[SM] * 3
        + full
        + [pl.BlockSpec((1, slots, 2, coeffs, coeffs), lambda n: (n, 0, 0, 0, 0))],
        out_specs=(VM,) * len(outs),
        scratch_shapes=[pltpu.VMEM((5 * spheres, 8, coeffs), F32)],
        cost_estimate=pl.CostEstimate(
            flops=2 * 8 * 2 * coeffs * coeffs * spheres * slots,
            bytes_accessed=blocks.size * 2,
            transcendentals=0,
        ),
    )(place, neighbours, live, *mine, *theirs, blocks)


def finish_kernel(
    place, box, list_mine, list_theirs, z0, z1, z2, z3, table_mine, table_theirs, turn, dis,
    near_mine, near_got, tmatrix, current, out, source, factor, field, local
):
    own_boxes, listed = list_mine.shape
    boxes = 2 * own_boxes
    waves = source.shape[2]
    spheres = tmatrix.shape[0]
    coeffs = tmatrix.shape[2]
    first = place[0] == 0
    total = jnp.zeros((2 * boxes, 2 * waves), F32)
    for part in (z0, z1, z2, z3):
        total += part[:, pl.ds(0, 2 * waves)].astype(F32)
    for r in range(2):
        re = total[r * boxes : (r + 1) * boxes, :waves]
        im = total[r * boxes : (r + 1) * boxes, waves:]
        source[:, r, :] = re
        source[:, 2 + r, :] = im
        source[:, 4 + r, :] = -im
        source[:, 6 + r, :] = re
    size = table_mine.shape[0]
    mine, theirs = table_mine[...].astype(F32), table_theirs[...].astype(F32)
    factor[pl.ds(0, size), :] = jnp.where(first, mine, theirs)
    factor[pl.ds(size, size), :] = jnp.where(first, theirs, mine)
    upper = lax.broadcasted_iota(jnp.int32, (8, waves), 0) < 4

    def one_box(b, carry):
        row = b % own_boxes
        is_mine = b // own_boxes == place[0]
        sums = [jnp.zeros((8, waves), F32) for _ in range(2)]
        for f in range(listed):
            which = jnp.where(is_mine, list_mine[row, f], list_theirs[row, f])
            at = (b * listed + f) * 2
            weight = jnp.where(upper, factor[pl.ds(at, 1), :], factor[pl.ds(at + 1, 1), :])
            sums[f % 2] = sums[f % 2] + weight * source[which]
        both = sums[0] + sums[1]
        field[b] = both[:4] + both[4:]
        return carry

    lax.fori_loop(box[0], box[spheres - 1] + 1, one_box, 0)
    for n in range(spheres):
        local[:, n, :] = field[box[n]]
    re = local[pl.ds(0, 2)].reshape(2 * spheres, waves)
    im = local[pl.ds(2, 2)].reshape(2 * spheres, waves)
    cosine = turn[pl.ds(0, 2 * spheres), pl.ds(0, waves)]
    sine = turn[pl.ds(0, 2 * spheres), pl.ds(waves, waves)]
    shifted = jnp.concatenate([re * cosine + im * sine, im * cosine - re * sine], axis=1)
    total = jnp.dot(shifted.astype(BF16), dis[...], preferred_element_type=F32)
    total += near_mine[...] + near_got[...]
    t_re = jnp.concatenate([tmatrix[:, 0], tmatrix[:, 0]], axis=0)
    t_im = jnp.concatenate([tmatrix[:, 1], tmatrix[:, 1]], axis=0)
    f_re, f_im = total[:, :coeffs], total[:, coeffs:]
    start = current[:, pl.ds(0, 2 * coeffs)].astype(F32)
    out[:, pl.ds(0, coeffs)] = (start[:, :coeffs] - (t_re * f_re - t_im * f_im)).astype(BF16)
    out[:, pl.ds(coeffs, coeffs)] = (start[:, coeffs:] - (t_re * f_im + t_im * f_re)).astype(BF16)


def join_kernel(place, mine, theirs, out):
    spheres = out.shape[0]
    first = place[0] == 0
    for r in range(2):
        own = mine[pl.ds(r * spheres, spheres), :].astype(F32)
        other = theirs[pl.ds(r * spheres, spheres), :].astype(F32)
        out[:, r, :] = jnp.where(first, own, other).astype(BF16)
        out[:, 2 + r, :] = jnp.where(first, other, own).astype(BF16)


def swap_far(block):
    return lax.ppermute(block, "far", [(0, 1), (1, 0)])


def kernel_shards(
    vectors, near_blocks, neighbours, live_counts, tmatrix, agg_matrix, sphere_box, agg_angle,
    far_list, far_factors, dis_matrix
):
    spheres, newton, width = vectors.shape
    coeffs = width // 2
    own_boxes, listed = far_list.shape
    boxes = 2 * own_boxes
    waves = agg_matrix.shape[1] // 2
    rows = spheres * newton // 2
    near_pos = lax.axis_index("near")
    place = jnp.stack([lax.axis_index("far"), near_pos % 4, near_pos // 4, near_pos])
    place = place.astype(jnp.int32)
    entries = own_boxes * listed * 2
    message = call(
        pack_kernel,
        [((rows, 1024 + waves + entries), BF16)],
        [SM, SM, VM, VM, VM],
        (place, sphere_box, vectors, agg_angle, far_factors.reshape(entries, -1)),
    )[0]
    list_theirs = swap_far(far_list)
    current, edge = message, edge_rows(message[:, :1024])
    table = None
    for step in range(2):
        if step == 0:
            parts = xor_gather(message, (1, 2, 3))
            block, turn, member, _ = call(
                functools.partial(first_waves_kernel, boxes),
                [
                    ((2 * boxes, 2 * waves + waves // 4 * entries // (2 * boxes)), BF16),
                    ((4 * rows, 2 * waves), F32),
                    ((4 * rows, 2 * boxes), BF16),
                    ((waves // 4, entries), F32),
                ],
                [SM] + [VM] * 5,
                (place, *parts, agg_matrix),
            )
        else:
            edge = edge_rows(current)
            parts = xor_gather(current, (1, 2, 3))
            block = call(
                next_waves_kernel,
                [((2 * boxes, 2 * waves), BF16)],
                [VM] * 7,
                (*parts, agg_matrix, turn, member),
            )[0]
        pieces = xor_gather(block, (4, 8, 12))
        mine = (*parts, edge)
        if step == 0:
            near_mine, near_theirs = near_call(
                (0, 512), False, place, neighbours, live_counts, mine, mine, near_blocks
            )
        else:
            theirs = swap_far(jnp.concatenate(mine, axis=0))
            near_mine, near_theirs, first_image = near_call(
                (0, None), True, place, neighbours, live_counts, mine, (theirs,), near_blocks
            )
        near_got = swap_far(near_theirs)
        if step == 0:
            table = call(
                functools.partial(table_kernel, waves),
                [((entries, waves), BF16)],
                [SM] + [VM] * 4,
                (place, *pieces),
                [pltpu.VMEM((waves, entries), F32)],
            )[0]
            table = (table, swap_far(table))
        current = call(
            finish_kernel,
            [((rows, width), BF16)],
            [SM] * 4 + [VM] * 12,
            (
                place, sphere_box, far_list, list_theirs, *pieces, *table, turn, dis_matrix,
                near_mine, near_got, tmatrix, current
            ),
            [
                pltpu.VMEM((boxes, 8, waves), F32),
                pltpu.VMEM((2 * entries, waves), F32),
                pltpu.VMEM((boxes, 4, waves), F32),
                pltpu.VMEM((4, spheres, waves), F32),
            ],
        )[0]
    second_image = call(
        join_kernel,
        [((spheres, newton, width), BF16)],
        [SM, VM, VM],
        (place, current, swap_far(current)),
    )[0]
    return first_image, second_image


def shards(*args):
    if lax.axis_size("near") == 16 and lax.axis_size("far") == 2:
        return kernel_shards(*args)
    return plain_shards(*args)


def solution(mesh):
    return jax.shard_map(
        shards,
        mesh=mesh,
        in_specs=(
            P("near", None, None),
            P("near", "far", None, None, None),
            P("near", "far"),
            P("near"),
            P("near", None, None),
            P(),
            P("near"),
            P("near", None),
            P("far", None),
            P("far", None, None, "near"),
            P(),
        ),
        out_specs=(P("near", None, None), P("near", None, None)),
        check_vma=False,
    )
```

```python
import functools

import jax
import jax.numpy as jnp
from jax import lax
from jax.experimental import pallas as pl
from jax.experimental.pallas import tpu as pltpu
from jax.sharding import PartitionSpec as P

F32 = jnp.float32
BF16 = jnp.bfloat16
RADIX = 4


def complex_mul(left_re, left_im, right_re, right_im):
    return (left_re * right_re - left_im * right_im, left_re * right_im + left_im * right_re)


def swap_near(block, mask):
    count = lax.axis_size("near")
    return lax.ppermute(block, "near", [(i, i ^ mask) for i in range(count)])


def phase_masks():
    count = lax.axis_size("near")
    phases, step = [], 1
    while step < count:
        radix = min(RADIX, count // step)
        phases.append([step * j for j in range(1, radix)])
        step *= radix
    return phases


def xor_gather(block, masks):
    return [block] + [swap_near(block, mask) for mask in masks]


def in_order(parts, masks):
    step = masks[0]
    digit = lax.axis_index("near") // step % len(parts)
    stacked = jnp.stack(parts)
    return jnp.take(stacked, jnp.arange(len(parts)) ^ digit, axis=0)


def edge_rows(block):
    count = lax.axis_size("near")
    pairs = []
    for low in range(RADIX, count, RADIX):
        pairs.append((low - 1, low))
        pairs.append((low, low - 1))
    return lax.ppermute(block, "near", pairs) if pairs else jnp.zeros_like(block)


def over_far(block):
    count = lax.axis_size("far")
    if count == 2:
        other = lax.ppermute(block, "far", [(0, 1), (1, 0)])
        first = lax.axis_index("far") == 0
        return jnp.stack([jnp.where(first, block, other), jnp.where(first, other, block)])
    return lax.all_gather(block, "far", axis=0)


def near_share(partial, share):
    count = lax.axis_size("far")
    far_pos = lax.axis_index("far")
    mine = lax.dynamic_slice_in_dim(partial, far_pos % (partial.shape[1] // share) * share, share, 1)
    if count == 2:
        theirs = lax.dynamic_slice_in_dim(partial, (1 - far_pos) * share, share, 1)
        return mine + lax.ppermute(theirs, "far", [(0, 1), (1, 0)])
    total = lax.psum(partial, "far")
    return lax.dynamic_slice_in_dim(total, far_pos % (partial.shape[1] // share) * share, share, 1)


def plain_shards(
    vectors,
    near_blocks,
    neighbours,
    live_counts,
    tmatrix,
    agg_matrix,
    sphere_box,
    agg_angle,
    far_list,
    far_factors,
    dis_matrix,
):
    spheres, newton, width = vectors.shape
    coeffs = width // 2
    slots = neighbours.shape[1]
    far_count = lax.axis_size("far")
    near_count = lax.axis_size("near")
    own_boxes, listed = far_list.shape
    boxes = own_boxes * far_count
    waves = agg_matrix.shape[1] // 2
    share = newton // min(far_count, newton)
    splits = newton // share
    near_pos = lax.axis_index("near")
    far_pos = lax.axis_index("far")
    phases = phase_masks()
    rows = spheres * share

    def own_share(block):
        return lax.dynamic_slice_in_dim(block, far_pos % splits * share, share, 1)

    rounded = lax.reduce_precision(agg_angle, 8, 7)
    hi, low = rounded.astype(BF16), (agg_angle - rounded).astype(BF16)
    factors = far_factors.astype(BF16).reshape(-1, far_factors.shape[-1]).T
    per_part = factors.size
    lists = over_far_lists(far_list)
    extra = jnp.concatenate(
        [
            jnp.repeat(sphere_box, share).astype(BF16)[:, None],
            jnp.stack([hi, low]).reshape(rows, -1),
            factors.reshape(rows, -1),
        ],
        axis=1,
    )
    angle_width = 2 * spheres * waves // rows

    cosine = jnp.cos(agg_angle)
    sine = jnp.sin(agg_angle)
    alive = (far_pos * slots + jnp.arange(slots, dtype=jnp.int32))[None, :] < live_counts[:, None]
    chip = neighbours // spheres
    place = jnp.where(chip // RADIX == near_pos // RADIX, chip ^ near_pos, RADIX)
    local_index = place * spheres + neighbours % spheres

    state = {}
    images = []
    current = own_share(vectors)
    whole = vectors
    for step in range(2):
        flat = current.reshape(rows, width)
        edge = edge_rows(current)
        message = jnp.concatenate([flat, extra], axis=1) if step == 0 else flat
        parts = xor_gather(message, phases[0])
        group = len(parts)
        around = [p[:, :width].reshape(spheres, share, width) for p in parts]
        full = over_far(jnp.stack(around + [edge]))[:splits]
        full = jnp.moveaxis(full, 0, 2).reshape((group + 1) * spheres, newton, width)
        if step == 1:
            images.append(full[:spheres])
        if step == 0:
            box_ids = jnp.concatenate([p[:, width].reshape(spheres, share)[:, 0] for p in parts])
            angles = jnp.stack(
                [
                    p[:, width + 1 : width + 1 + angle_width].reshape(2, spheres, waves)
                    for p in parts
                ]
            ).astype(F32)
            angles = (angles[:, 0] + angles[:, 1]).reshape(group * spheres, waves)
            state["cos"], state["sin"] = jnp.cos(angles), jnp.sin(angles)
            state["member"] = (
                box_ids.astype(jnp.int32)[None, :] == jnp.arange(boxes, dtype=jnp.int32)[:, None]
            ).astype(F32)
            table = in_order([p[:, width + 1 + angle_width :] for p in parts], phases[0])
        product = jnp.dot(
            jnp.concatenate(around).reshape(group * rows, width),
            agg_matrix,
            preferred_element_type=F32,
        ).reshape(group * spheres, share, 2, waves)
        out_re, out_im = complex_mul(
            product[:, :, 0], product[:, :, 1], state["cos"][:, None], state["sin"][:, None]
        )
        stacked = jnp.concatenate([out_re, out_im], axis=-1)
        sums = jnp.einsum("bn,nrq->brq", state["member"], stacked, precision=lax.Precision.HIGHEST)
        for masks in phases[1:]:
            block = sums.astype(BF16).reshape(boxes * share, 2 * waves)
            if step == 0:
                block = jnp.concatenate([block, table.reshape(boxes * share, -1)], axis=1)
            pieces = xor_gather(block, masks)
            sums = sum(p[:, : 2 * waves].astype(F32) for p in pieces)
            sums = sums.reshape(boxes, share, 2 * waves)
            if step == 0:
                table = in_order([p[:, 2 * waves :] for p in pieces], masks)
        if step == 0:
            table = over_far(table.reshape(waves, own_boxes, listed, 2))
            table = table.transpose(0, 2, 3, 4, 1).reshape(boxes, listed, 2, waves)
            state["factors"] = table[sphere_box].astype(F32)
            state["sources"] = (
                lists[sphere_box][:, :, None] == jnp.arange(boxes, dtype=jnp.int32)
            ).astype(F32)
        gathered = jnp.where(alive[:, :, None, None], full[local_index], jnp.zeros((), BF16))
        both = jnp.concatenate([gathered[..., :coeffs], gathered[..., coeffs:]], axis=2)
        with_real = jnp.einsum(
            "nkrc,nkcd->nrd", both, near_blocks[:, :, 0], preferred_element_type=F32
        )
        with_imag = jnp.einsum(
            "nkrc,nkcd->nrd", both, near_blocks[:, :, 1], preferred_element_type=F32
        )
        near_re = with_real[:, :newton] - with_imag[:, newton:]
        near_im = with_imag[:, :newton] + with_real[:, newton:]
        near_field = near_share(jnp.concatenate([near_re, near_im], axis=-1), share)
        picked = jnp.einsum(
            "nfb,brq->nfrq", state["sources"], sums, precision=lax.Precision.HIGHEST
        )
        fac = state["factors"]
        in_re, in_im = complex_mul(
            fac[:, :, None, 0], fac[:, :, None, 1], picked[..., :waves], picked[..., waves:]
        )
        in_re, in_im = jnp.sum(in_re, axis=1), jnp.sum(in_im, axis=1)
        local_re, local_im = complex_mul(in_re, in_im, cosine[:, None], -sine[:, None])
        local_waves = jnp.concatenate([local_re, local_im], axis=-1).astype(BF16)
        far_field = jnp.dot(
            local_waves.reshape(rows, 2 * waves), dis_matrix, preferred_element_type=F32
        ).reshape(spheres, share, width)
        field = near_field + far_field
        scat_re, scat_im = complex_mul(
            tmatrix[:, None, 0], tmatrix[:, None, 1], field[..., :coeffs], field[..., coeffs:]
        )
        current = (current.astype(F32) - jnp.concatenate([scat_re, scat_im], axis=-1)).astype(BF16)
    last = over_far(current)[:splits]
    images.append(jnp.moveaxis(last, 0, 1).reshape(spheres, newton, width))
    return tuple(images)


def over_far_lists(far_list):
    gathered = over_far(far_list)
    return gathered.reshape(-1, far_list.shape[1])


VM = pl.BlockSpec(memory_space=pltpu.VMEM)
SM = pl.BlockSpec(memory_space=pltpu.SMEM)


def call(kernel, outs, specs, args, scratch=(), flops=0, moved=6 << 20, limit=4 << 20):
    return pl.pallas_call(
        kernel,
        out_shape=tuple(jax.ShapeDtypeStruct(shape, kind) for shape, kind in outs),
        in_specs=list(specs),
        out_specs=(VM,) * len(outs),
        scratch_shapes=list(scratch),
        cost_estimate=pl.CostEstimate(flops=flops, bytes_accessed=moved, transcendentals=0),
        compiler_params=pltpu.CompilerParams(vmem_limit_bytes=limit),
    )(*args)


def here():
    near_pos = lax.axis_index("near")
    return lax.axis_index("far"), near_pos % 4, near_pos // 4, near_pos


def pack_kernel(box, vectors, angle, factors, out, edge):
    place = here()
    spheres, newton, width = vectors.shape
    share = newton // 2
    waves = angle.shape[1]
    first = place[0] == 0
    values = vectors[...].astype(F32)
    for r in range(share):
        low, high = values[:, r], values[:, share + r]
        rows = pl.ds(r * spheres, spheres)
        out[rows, pl.ds(0, width)] = jnp.where(first, low, high).astype(BF16)
        out[rows, pl.ds(512, width)] = jnp.where(first, high, low).astype(BF16)
    lane = lax.broadcasted_iota(jnp.int32, (spheres * share, 512 - width), 0) % spheres
    ids = jnp.zeros((spheres * share, 512 - width), F32)
    for n in range(spheres):
        ids = jnp.where(lane == n, box[n].astype(F32), ids)
    out[:, pl.ds(width, 512 - width)] = ids.astype(BF16)
    hi = angle[...].astype(BF16)
    low = (angle[...] - hi.astype(F32)).astype(BF16)
    out[pl.ds(0, spheres), pl.ds(1024, waves)] = hi
    out[pl.ds(spheres, spheres), pl.ds(1024, waves)] = low
    out[:, pl.ds(1024 + waves, factors.shape[0])] = factors[...].T.astype(BF16)
    edge[...] = out[:, pl.ds(0, 1024)]


def sum_rows(member, waves):
    dims = (((0,), (0,)), ((), ()))
    hi = waves.astype(BF16)
    low = (waves - hi.astype(F32)).astype(BF16)
    return lax.dot_general(member, hi, dims, preferred_element_type=F32) + lax.dot_general(
        member, low, dims, preferred_element_type=F32
    )


def turned(product, turn, waves):
    cosine, sine = turn[:, :waves], turn[:, waves:]
    re, im = product[:, :waves], product[:, waves:]
    return jnp.concatenate([re * cosine - im * sine, re * sine + im * cosine], axis=1)


def first_waves_kernel(boxes, p0, p1, p2, p3, agg, out, turn, member, table):
    place = here()
    parts = (p0, p1, p2, p3)
    width = agg.shape[0]
    waves = agg.shape[1] // 2
    rows = p0.shape[0]
    half = rows // 2
    held = table.shape[0] // 4
    for j, part in enumerate(parts):
        angle = part[pl.ds(0, half), pl.ds(1024, waves)].astype(F32)
        angle += part[pl.ds(half, half), pl.ds(1024, waves)].astype(F32)
        both = jnp.concatenate([jnp.cos(angle), jnp.sin(angle)], axis=1)
        turn[pl.ds(j * rows, half), :] = both
        turn[pl.ds(j * rows + half, half), :] = both
        ids = part[:, pl.ds(width, 1)].astype(F32)
        row = lax.broadcasted_iota(jnp.int32, (rows, 2 * boxes), 0) // half
        col = lax.broadcasted_iota(jnp.int32, (rows, 2 * boxes), 1)
        hit = (ids == (col % boxes).astype(F32)) & (row == col // boxes)
        member[pl.ds(j * rows, rows), :] = jnp.where(hit, 1.0, 0.0).astype(BF16)
        at = pl.multiple_of((place[1] ^ j) * held, held)
        table[pl.ds(at, held), :] = part[:, pl.ds(1024 + waves, table.shape[1])].astype(F32)
    flat = jnp.concatenate([p[:, pl.ds(0, width)] for p in parts], axis=0)
    product = jnp.dot(flat, agg[...], preferred_element_type=F32)
    sums = sum_rows(member[...], turned(product, turn[...], waves))
    out[:, pl.ds(0, 2 * waves)] = sums.astype(BF16)
    lines = out.shape[0]
    span = table.shape[1]
    for j in range(table.shape[0] // lines):
        out[:, pl.ds(2 * waves + j * span, span)] = table[pl.ds(j * lines, lines), :].astype(BF16)


def next_waves_kernel(p0, p1, p2, p3, p4, agg, turn, member, out, around):
    waves = agg.shape[1] // 2
    rows = p0.shape[0]
    for j, part in enumerate((p0, p1, p2, p3, p4)):
        around[pl.ds(j * rows, rows), :] = part[...]
    flat = jnp.concatenate([p0[...], p1[...], p2[...], p3[...]], axis=0)
    product = jnp.dot(flat, agg[...], preferred_element_type=F32)
    out[...] = sum_rows(member[...], turned(product, turn[...], waves)).astype(BF16)


def table_kernel(waves, z0, z1, z2, z3, out, held):
    place = here()
    lines = z0.shape[0]
    span = held.shape[1]
    pieces = (z0.shape[1] - 2 * waves) // span
    for j, part in enumerate((z0, z1, z2, z3)):
        for i in range(pieces):
            at = pl.multiple_of(((place[2] ^ j) * pieces + i) * lines, lines)
            held[pl.ds(at, lines), :] = part[:, pl.ds(2 * waves + i * span, span)].astype(F32)
    out[...] = held[...].T.astype(BF16)


def near_kernel(starts, emit, neighbours, live, *refs):
    place = here()
    mine, theirs = refs[:5], refs[5 : 5 + (5 if starts[1] is not None else 1)]
    refs = refs[5 + len(theirs) :]
    blocks = refs[0]
    out_mine, out_theirs = refs[1], refs[2]
    image = refs[3] if emit else None
    held = refs[4]
    if not emit:
        source_blocks, blocks, arrived = blocks, refs[3], refs[5]
        copies = [
            pltpu.make_async_copy(source_blocks.at[n], blocks.at[n], arrived.at[n])
            for n in range(blocks.shape[0])
        ]
        for copy in copies:
            copy.start()
    spheres = out_mine.shape[0] // 2
    slots = blocks.shape[1]
    coeffs = blocks.shape[3]
    for j in range(5):
        for side in range(2):
            for r in range(2):
                rows = pl.ds(r * spheres, spheres)
                if side == 0:
                    value = mine[j][rows, pl.ds(0, 2 * coeffs)]
                elif starts[1] is not None:
                    value = theirs[j][rows, pl.ds(starts[1], 2 * coeffs)]
                else:
                    value = theirs[0][pl.ds((2 * j + r) * spheres, spheres), :]
                value = value.astype(F32)
                at = pl.ds(j * spheres, spheres)
                held[at, side * 2 + r, :] = value[:, :coeffs]
                held[at, 4 + side * 2 + r, :] = value[:, coeffs:]
    if emit:
        first = place[0] == 0
        for r in range(2):
            own = mine[0][pl.ds(r * spheres, spheres), :].astype(F32)
            other = theirs[0][pl.ds(r * spheres, spheres), :].astype(F32)
            image[:, r, :] = jnp.where(first, own, other).astype(BF16)
            image[:, 2 + r, :] = jnp.where(first, other, own).astype(BF16)

    for n in range(spheres):
        real = jnp.zeros((8, coeffs), F32)
        imag = jnp.zeros((8, coeffs), F32)
        if not emit:
            copies[n].wait()
        for k in range(slots):
            source = neighbours[n, k]
            chip = source // spheres
            near = jnp.where(chip // 4 == place[3] // 4, chip ^ place[3], 4)
            value = held[near * spheres + source % spheres]
            alive = place[0] * slots + k < live[n]
            value = jnp.where(alive, value, 0.0).astype(BF16)
            real += jnp.dot(value, blocks[n, k, 0], preferred_element_type=F32)
            imag += jnp.dot(value, blocks[n, k, 1], preferred_element_type=F32)
        near_re = real[:4] - imag[4:]
        near_im = imag[:4] + real[4:]
        for r in range(2):
            row = pl.ds(r * spheres + n, 1)
            out_mine[row, pl.ds(0, coeffs)] = near_re[r : r + 1]
            out_mine[row, pl.ds(coeffs, coeffs)] = near_im[r : r + 1]
            out_theirs[row, pl.ds(0, coeffs)] = near_re[2 + r : 3 + r]
            out_theirs[row, pl.ds(coeffs, coeffs)] = near_im[2 + r : 3 + r]


def near_call(starts, emit, neighbours, live, mine, theirs, blocks):
    spheres, slots, _, coeffs, _ = blocks.shape
    rows = 2 * spheres
    outs = [jax.ShapeDtypeStruct((rows, 2 * coeffs), F32)] * 2
    if emit:
        outs.append(jax.ShapeDtypeStruct((spheres, 4, 2 * coeffs), BF16))
    else:
        outs.append(pltpu.VMEM(blocks.shape, BF16))
    full = [VM] * (len(mine) + len(theirs))
    return pl.pallas_call(
        functools.partial(near_kernel, starts, emit),
        out_shape=tuple(outs),
        in_specs=[SM] * 2 + full + [VM if emit else pl.BlockSpec(memory_space=pl.ANY)],
        out_specs=(VM,) * len(outs),
        scratch_shapes=[pltpu.VMEM((5 * spheres, 8, coeffs), F32)]
        + ([] if emit else [pltpu.SemaphoreType.DMA((spheres,))]),
        cost_estimate=pl.CostEstimate(
            flops=2 * 8 * 2 * coeffs * coeffs * spheres * slots,
            bytes_accessed=blocks.size * 2,
            transcendentals=0,
        ),
        compiler_params=pltpu.CompilerParams(vmem_limit_bytes=(4 if emit else 34) << 20),
    )(neighbours, live, *mine, *theirs, blocks)


def finish_kernel(
    box, list_mine, list_theirs, z0, z1, z2, z3, table_mine, table_theirs, turn, dis,
    near_mine, near_got, tmatrix, current, out, source, factor, field, local
):
    place = here()
    own_boxes, listed = list_mine.shape
    boxes = 2 * own_boxes
    waves = source.shape[2]
    spheres = tmatrix.shape[0]
    coeffs = tmatrix.shape[2]
    first = place[0] == 0
    total = jnp.zeros((2 * boxes, 2 * waves), F32)
    for part in (z0, z1, z2, z3):
        total += part[:, pl.ds(0, 2 * waves)].astype(F32)
    for r in range(2):
        re = total[r * boxes : (r + 1) * boxes, :waves]
        im = total[r * boxes : (r + 1) * boxes, waves:]
        source[:, r, :] = re
        source[:, 2 + r, :] = im
        source[:, 4 + r, :] = -im
        source[:, 6 + r, :] = re
    size = table_mine.shape[0]
    mine, theirs = table_mine[...].astype(F32), table_theirs[...].astype(F32)
    factor[pl.ds(0, size), :] = jnp.where(first, mine, theirs)
    factor[pl.ds(size, size), :] = jnp.where(first, theirs, mine)
    upper = lax.broadcasted_iota(jnp.int32, (8, waves), 0) < 4

    def one_box(b, carry):
        row = b % own_boxes
        is_mine = b // own_boxes == place[0]
        sums = [jnp.zeros((8, waves), F32) for _ in range(2)]
        for f in range(listed):
            which = jnp.where(is_mine, list_mine[row, f], list_theirs[row, f])
            at = (b * listed + f) * 2
            weight = jnp.where(upper, factor[pl.ds(at, 1), :], factor[pl.ds(at + 1, 1), :])
            sums[f % 2] = sums[f % 2] + weight * source[which]
        both = sums[0] + sums[1]
        field[b] = both[:4] + both[4:]
        return carry

    lax.fori_loop(box[0], box[spheres - 1] + 1, one_box, 0)
    for n in range(spheres):
        local[:, n, :] = field[box[n]]
    re = local[pl.ds(0, 2)].reshape(2 * spheres, waves)
    im = local[pl.ds(2, 2)].reshape(2 * spheres, waves)
    cosine = turn[pl.ds(0, 2 * spheres), pl.ds(0, waves)]
    sine = turn[pl.ds(0, 2 * spheres), pl.ds(waves, waves)]
    shifted = jnp.concatenate([re * cosine + im * sine, im * cosine - re * sine], axis=1)
    dims = (((1,), (1,)), ((), ()))
    total = lax.dot_general(shifted.astype(BF16), dis[...], dims, preferred_element_type=F32)
    total += near_mine[...] + near_got[...]
    t_re = jnp.concatenate([tmatrix[:, 0], tmatrix[:, 0]], axis=0)
    t_im = jnp.concatenate([tmatrix[:, 1], tmatrix[:, 1]], axis=0)
    f_re, f_im = total[:, :coeffs], total[:, coeffs:]
    start = current[:, pl.ds(0, 2 * coeffs)].astype(F32)
    out[:, pl.ds(0, coeffs)] = (start[:, :coeffs] - (t_re * f_re - t_im * f_im)).astype(BF16)
    out[:, pl.ds(coeffs, coeffs)] = (start[:, coeffs:] - (t_re * f_im + t_im * f_re)).astype(BF16)


def join_kernel(mine, theirs, out):
    spheres = out.shape[0]
    first = lax.axis_index("far") == 0
    for r in range(2):
        own = mine[pl.ds(r * spheres, spheres), :].astype(F32)
        other = theirs[pl.ds(r * spheres, spheres), :].astype(F32)
        out[:, r, :] = jnp.where(first, own, other).astype(BF16)
        out[:, 2 + r, :] = jnp.where(first, other, own).astype(BF16)


def swap_far(block):
    return lax.ppermute(block, "far", [(0, 1), (1, 0)])


def kernel_shards(
    vectors, near_blocks, neighbours, live_counts, tmatrix, agg_matrix, sphere_box, agg_angle,
    far_list, far_factors, dis_matrix
):
    spheres, newton, width = vectors.shape
    coeffs = width // 2
    own_boxes, listed = far_list.shape
    boxes = 2 * own_boxes
    waves = agg_matrix.shape[1] // 2
    rows = spheres * newton // 2
    entries = own_boxes * listed * 2
    message, edge = call(
        pack_kernel,
        [((rows, 1024 + waves + entries), BF16), ((rows, 1024), BF16)],
        [SM, VM, VM, VM],
        (sphere_box, vectors, agg_angle, far_factors.reshape(entries, -1)),
    )
    list_theirs = swap_far(far_list)
    current, edge = message, edge_rows(edge)
    table = None
    for step in range(2):
        if step == 0:
            parts = xor_gather(message, (1, 2, 3))
            parts, edge, list_theirs = lax.optimization_barrier((parts, edge, list_theirs))
            block, turn, member, _ = call(
                functools.partial(first_waves_kernel, boxes),
                [
                    ((2 * boxes, 2 * waves + waves // 4 * entries // (2 * boxes)), BF16),
                    ((4 * rows, 2 * waves), F32),
                    ((4 * rows, 2 * boxes), BF16),
                    ((waves // 4, entries), F32),
                ],
                [VM] * 5,
                (*parts, agg_matrix),
            )
        else:
            edge = edge_rows(current)
            parts = xor_gather(current, (1, 2, 3))
            block, around = call(
                next_waves_kernel,
                [((2 * boxes, 2 * waves), BF16), ((5 * rows, width), BF16)],
                [VM] * 8,
                (*parts, edge, agg_matrix, turn, member),
            )
        pieces = xor_gather(block, (4, 8, 12))
        mine = (*parts, edge)
        if step == 0:
            near_mine, near_theirs, held_blocks = near_call(
                (0, 512), False, neighbours, live_counts, mine, mine, near_blocks
            )
        else:
            theirs = swap_far(around)
            near_mine, near_theirs, first_image = near_call(
                (0, None), True, neighbours, live_counts, mine, (theirs,), held_blocks
            )
        near_got = swap_far(near_theirs)
        if step == 0:
            pieces, near_mine = lax.optimization_barrier((pieces, near_mine))
            table = call(
                functools.partial(table_kernel, waves),
                [((entries, waves), BF16)],
                [VM] * 4,
                (*pieces,),
                [pltpu.VMEM((waves, entries), F32)],
            )[0]
            table = (table, swap_far(table))
        current = call(
            finish_kernel,
            [((rows, width), BF16)],
            [SM] * 3 + [VM] * 12,
            (
                sphere_box, far_list, list_theirs, *pieces, *table, turn, dis_matrix.T,
                near_mine, near_got, tmatrix, current
            ),
            [
                pltpu.VMEM((boxes, 8, waves), F32),
                pltpu.VMEM((2 * entries, waves), F32),
                pltpu.VMEM((boxes, 4, waves), F32),
                pltpu.VMEM((4, spheres, waves), F32),
            ],
        )[0]
    second_image = call(
        join_kernel,
        [((spheres, newton, width), BF16)],
        [VM, VM],
        (current, swap_far(current)),
    )[0]
    return first_image, second_image


def shards(*args):
    if lax.axis_size("near") == 16 and lax.axis_size("far") == 2:
        return kernel_shards(*args)
    return plain_shards(*args)


def solution(mesh):
    return jax.shard_map(
        shards,
        mesh=mesh,
        in_specs=(
            P("near", None, None),
            P("near", "far", None, None, None),
            P("near", "far"),
            P("near"),
            P("near", None, None),
            P(),
            P("near"),
            P("near", None),
            P("far", None),
            P("far", None, None, "near"),
            P(),
        ),
        out_specs=(P("near", None, None), P("near", None, None)),
        check_vma=False,
    )
```

```python
import functools

import jax
import jax.numpy as jnp
from jax import lax
from jax.experimental import pallas as pl
from jax.experimental.pallas import tpu as pltpu
from jax.sharding import PartitionSpec as P

F32 = jnp.float32
BF16 = jnp.bfloat16
RADIX = 4


def complex_mul(left_re, left_im, right_re, right_im):
    return (left_re * right_re - left_im * right_im, left_re * right_im + left_im * right_re)


def swap_near(block, mask):
    count = lax.axis_size("near")
    return lax.ppermute(block, "near", [(i, i ^ mask) for i in range(count)])


def phase_masks():
    count = lax.axis_size("near")
    phases, step = [], 1
    while step < count:
        radix = min(RADIX, count // step)
        phases.append([step * j for j in range(1, radix)])
        step *= radix
    return phases


def xor_gather(block, masks):
    return [block] + [swap_near(block, mask) for mask in masks]


def in_order(parts, masks):
    step = masks[0]
    digit = lax.axis_index("near") // step % len(parts)
    stacked = jnp.stack(parts)
    return jnp.take(stacked, jnp.arange(len(parts)) ^ digit, axis=0)


def edge_rows(block):
    count = lax.axis_size("near")
    pairs = []
    for low in range(RADIX, count, RADIX):
        pairs.append((low - 1, low))
        pairs.append((low, low - 1))
    return lax.ppermute(block, "near", pairs) if pairs else jnp.zeros_like(block)


def over_far(block):
    count = lax.axis_size("far")
    if count == 2:
        other = lax.ppermute(block, "far", [(0, 1), (1, 0)])
        first = lax.axis_index("far") == 0
        return jnp.stack([jnp.where(first, block, other), jnp.where(first, other, block)])
    return lax.all_gather(block, "far", axis=0)


def near_share(partial, share):
    count = lax.axis_size("far")
    far_pos = lax.axis_index("far")
    mine = lax.dynamic_slice_in_dim(partial, far_pos % (partial.shape[1] // share) * share, share, 1)
    if count == 2:
        theirs = lax.dynamic_slice_in_dim(partial, (1 - far_pos) * share, share, 1)
        return mine + lax.ppermute(theirs, "far", [(0, 1), (1, 0)])
    total = lax.psum(partial, "far")
    return lax.dynamic_slice_in_dim(total, far_pos % (partial.shape[1] // share) * share, share, 1)


def plain_shards(
    vectors,
    near_blocks,
    neighbours,
    live_counts,
    tmatrix,
    agg_matrix,
    sphere_box,
    agg_angle,
    far_list,
    far_factors,
    dis_matrix,
):
    spheres, newton, width = vectors.shape
    coeffs = width // 2
    slots = neighbours.shape[1]
    far_count = lax.axis_size("far")
    own_boxes, listed = far_list.shape
    boxes = own_boxes * far_count
    waves = agg_matrix.shape[1] // 2
    share = newton // min(far_count, newton)
    splits = newton // share
    near_pos = lax.axis_index("near")
    far_pos = lax.axis_index("far")
    phases = phase_masks()
    rows = spheres * share

    def own_share(block):
        return lax.dynamic_slice_in_dim(block, far_pos % splits * share, share, 1)

    rounded = lax.reduce_precision(agg_angle, 8, 7)
    hi, low = rounded.astype(BF16), (agg_angle - rounded).astype(BF16)
    factors = far_factors.astype(BF16).reshape(-1, far_factors.shape[-1]).T
    lists = over_far_lists(far_list)
    extra = jnp.concatenate(
        [
            jnp.repeat(sphere_box, share).astype(BF16)[:, None],
            jnp.stack([hi, low]).reshape(rows, -1),
            factors.reshape(rows, -1),
        ],
        axis=1,
    )
    angle_width = 2 * spheres * waves // rows

    cosine = jnp.cos(agg_angle)
    sine = jnp.sin(agg_angle)
    alive = (far_pos * slots + jnp.arange(slots, dtype=jnp.int32))[None, :] < live_counts[:, None]
    chip = neighbours // spheres
    place = jnp.where(chip // RADIX == near_pos // RADIX, chip ^ near_pos, RADIX)
    local_index = place * spheres + neighbours % spheres

    state = {}
    images = []
    current = own_share(vectors)
    for step in range(2):
        flat = current.reshape(rows, width)
        edge = edge_rows(current)
        message = jnp.concatenate([flat, extra], axis=1) if step == 0 else flat
        parts = xor_gather(message, phases[0])
        group = len(parts)
        around = [p[:, :width].reshape(spheres, share, width) for p in parts]
        full = over_far(jnp.stack(around + [edge]))[:splits]
        full = jnp.moveaxis(full, 0, 2).reshape((group + 1) * spheres, newton, width)
        if step == 1:
            images.append(full[:spheres])
        if step == 0:
            box_ids = jnp.concatenate([p[:, width].reshape(spheres, share)[:, 0] for p in parts])
            angles = jnp.stack(
                [
                    p[:, width + 1 : width + 1 + angle_width].reshape(2, spheres, waves)
                    for p in parts
                ]
            ).astype(F32)
            angles = (angles[:, 0] + angles[:, 1]).reshape(group * spheres, waves)
            state["cos"], state["sin"] = jnp.cos(angles), jnp.sin(angles)
            state["member"] = (
                box_ids.astype(jnp.int32)[None, :] == jnp.arange(boxes, dtype=jnp.int32)[:, None]
            ).astype(F32)
            table = in_order([p[:, width + 1 + angle_width :] for p in parts], phases[0])
        product = jnp.dot(
            jnp.concatenate(around).reshape(group * rows, width),
            agg_matrix,
            preferred_element_type=F32,
        ).reshape(group * spheres, share, 2, waves)
        out_re, out_im = complex_mul(
            product[:, :, 0], product[:, :, 1], state["cos"][:, None], state["sin"][:, None]
        )
        stacked = jnp.concatenate([out_re, out_im], axis=-1)
        sums = jnp.einsum("bn,nrq->brq", state["member"], stacked, precision=lax.Precision.HIGHEST)
        for masks in phases[1:]:
            block = sums.astype(BF16).reshape(boxes * share, 2 * waves)
            if step == 0:
                block = jnp.concatenate([block, table.reshape(boxes * share, -1)], axis=1)
            pieces = xor_gather(block, masks)
            sums = sum(p[:, : 2 * waves].astype(F32) for p in pieces)
            sums = sums.reshape(boxes, share, 2 * waves)
            if step == 0:
                table = in_order([p[:, 2 * waves :] for p in pieces], masks)
        if step == 0:
            table = over_far(table.reshape(waves, own_boxes, listed, 2))
            table = table.transpose(0, 2, 3, 4, 1).reshape(boxes, listed, 2, waves)
            state["factors"] = table[sphere_box].astype(F32)
            state["sources"] = (
                lists[sphere_box][:, :, None] == jnp.arange(boxes, dtype=jnp.int32)
            ).astype(F32)
        gathered = jnp.where(alive[:, :, None, None], full[local_index], jnp.zeros((), BF16))
        both = jnp.concatenate([gathered[..., :coeffs], gathered[..., coeffs:]], axis=2)
        with_real = jnp.einsum(
            "nkrc,nkcd->nrd", both, near_blocks[:, :, 0], preferred_element_type=F32
        )
        with_imag = jnp.einsum(
            "nkrc,nkcd->nrd", both, near_blocks[:, :, 1], preferred_element_type=F32
        )
        near_re = with_real[:, :newton] - with_imag[:, newton:]
        near_im = with_imag[:, :newton] + with_real[:, newton:]
        near_field = near_share(jnp.concatenate([near_re, near_im], axis=-1), share)
        picked = jnp.einsum(
            "nfb,brq->nfrq", state["sources"], sums, precision=lax.Precision.HIGHEST
        )
        fac = state["factors"]
        in_re, in_im = complex_mul(
            fac[:, :, None, 0], fac[:, :, None, 1], picked[..., :waves], picked[..., waves:]
        )
        in_re, in_im = jnp.sum(in_re, axis=1), jnp.sum(in_im, axis=1)
        local_re, local_im = complex_mul(in_re, in_im, cosine[:, None], -sine[:, None])
        local_waves = jnp.concatenate([local_re, local_im], axis=-1).astype(BF16)
        far_field = jnp.dot(
            local_waves.reshape(rows, 2 * waves), dis_matrix, preferred_element_type=F32
        ).reshape(spheres, share, width)
        field = near_field + far_field
        scat_re, scat_im = complex_mul(
            tmatrix[:, None, 0], tmatrix[:, None, 1], field[..., :coeffs], field[..., coeffs:]
        )
        current = (current.astype(F32) - jnp.concatenate([scat_re, scat_im], axis=-1)).astype(BF16)
    last = over_far(current)[:splits]
    images.append(jnp.moveaxis(last, 0, 1).reshape(spheres, newton, width))
    return tuple(images)


def over_far_lists(far_list):
    gathered = over_far(far_list)
    return gathered.reshape(-1, far_list.shape[1])


VM = pl.BlockSpec(memory_space=pltpu.VMEM)
SM = pl.BlockSpec(memory_space=pltpu.SMEM)
HB = pl.BlockSpec(memory_space=pl.ANY)


def call(kernel, outs, specs, args, scratch=(), flops=0, moved=6 << 20, limit=4 << 20, held=False):
    make = pltpu.VMEM if held else jax.ShapeDtypeStruct
    return pl.pallas_call(
        kernel,
        out_shape=tuple(make(shape, kind) for shape, kind in outs),
        in_specs=list(specs),
        out_specs=(VM,) * len(outs),
        scratch_shapes=list(scratch),
        cost_estimate=pl.CostEstimate(flops=flops, bytes_accessed=moved, transcendentals=0),
        compiler_params=pltpu.CompilerParams(vmem_limit_bytes=limit),
    )(*args)


def here():
    near_pos = lax.axis_index("near")
    return lax.axis_index("far"), near_pos % 4, near_pos // 4, near_pos


def pack_kernel(box, vectors, angle, factors, *refs):
    out, edge = refs[-2:]
    place = here()
    spheres, newton, width = vectors.shape
    share = newton // 2
    waves = angle.shape[1]
    first = place[0] == 0
    values = vectors[...].astype(F32)
    for r in range(share):
        low, high = values[:, r], values[:, share + r]
        rows = pl.ds(r * spheres, spheres)
        out[rows, pl.ds(0, width)] = jnp.where(first, low, high).astype(BF16)
        out[rows, pl.ds(512, width)] = jnp.where(first, high, low).astype(BF16)
    lane = lax.broadcasted_iota(jnp.int32, (spheres * share, 512 - width), 0) % spheres
    ids = jnp.zeros((spheres * share, 512 - width), F32)
    for n in range(spheres):
        ids = jnp.where(lane == n, box[n].astype(F32), ids)
    out[:, pl.ds(width, 512 - width)] = ids.astype(BF16)
    hi = angle[...].astype(BF16)
    low = (angle[...] - hi.astype(F32)).astype(BF16)
    out[pl.ds(0, spheres), pl.ds(1024, waves)] = hi
    out[pl.ds(spheres, spheres), pl.ds(1024, waves)] = low
    out[:, pl.ds(1024 + waves, factors.shape[0])] = factors[...].T.astype(BF16)
    edge[...] = out[:, pl.ds(0, 1024)]


def sum_rows(member, waves):
    dims = (((0,), (0,)), ((), ()))
    hi = waves.astype(BF16)
    low = (waves - hi.astype(F32)).astype(BF16)
    return lax.dot_general(member, hi, dims, preferred_element_type=F32) + lax.dot_general(
        member, low, dims, preferred_element_type=F32
    )


def turned(product, turn, waves):
    cosine, sine = turn[:, :waves], turn[:, waves:]
    re, im = product[:, :waves], product[:, waves:]
    return jnp.concatenate([re * cosine - im * sine, re * sine + im * cosine], axis=1)


def first_waves_kernel(boxes, p0, p1, p2, p3, agg, out, turn, member, table):
    place = here()
    parts = (p0, p1, p2, p3)
    width = agg.shape[0]
    waves = agg.shape[1] // 2
    rows = p0.shape[0]
    half = rows // 2
    held = table.shape[0] // 4
    for j, part in enumerate(parts):
        angle = part[pl.ds(0, half), pl.ds(1024, waves)].astype(F32)
        angle += part[pl.ds(half, half), pl.ds(1024, waves)].astype(F32)
        both = jnp.concatenate([jnp.cos(angle), jnp.sin(angle)], axis=1)
        turn[pl.ds(j * rows, half), :] = both
        turn[pl.ds(j * rows + half, half), :] = both
        ids = part[:, pl.ds(width, 1)].astype(F32)
        row = lax.broadcasted_iota(jnp.int32, (rows, 2 * boxes), 0) // half
        col = lax.broadcasted_iota(jnp.int32, (rows, 2 * boxes), 1)
        hit = (ids == (col % boxes).astype(F32)) & (row == col // boxes)
        member[pl.ds(j * rows, rows), :] = jnp.where(hit, 1.0, 0.0).astype(BF16)
        at = pl.multiple_of((place[1] ^ j) * held, held)
        table[pl.ds(at, held), :] = part[:, pl.ds(1024 + waves, table.shape[1])].astype(F32)
    flat = jnp.concatenate([p[:, pl.ds(0, width)] for p in parts], axis=0)
    product = jnp.dot(flat, agg[...], preferred_element_type=F32)
    sums = sum_rows(member[...], turned(product, turn[...], waves))
    out[:, pl.ds(0, 2 * waves)] = sums.astype(BF16)
    lines = out.shape[0]
    span = table.shape[1]
    for j in range(table.shape[0] // lines):
        out[:, pl.ds(2 * waves + j * span, span)] = table[pl.ds(j * lines, lines), :].astype(BF16)


def next_waves_kernel(p0, p1, p2, p3, p4, agg, turn, member, out, around):
    waves = agg.shape[1] // 2
    rows = p0.shape[0]
    for j, part in enumerate((p0, p1, p2, p3, p4)):
        around[pl.ds(j * rows, rows), :] = part[...]
    flat = jnp.concatenate([p0[...], p1[...], p2[...], p3[...]], axis=0)
    product = jnp.dot(flat, agg[...], preferred_element_type=F32)
    out[...] = sum_rows(member[...], turned(product, turn[...], waves)).astype(BF16)


def table_kernel(waves, z0, z1, z2, z3, out, held):
    place = here()
    lines = z0.shape[0]
    span = held.shape[1]
    pieces = (z0.shape[1] - 2 * waves) // span
    for j, part in enumerate((z0, z1, z2, z3)):
        for i in range(pieces):
            at = pl.multiple_of(((place[2] ^ j) * pieces + i) * lines, lines)
            held[pl.ds(at, lines), :] = part[:, pl.ds(2 * waves + i * span, span)].astype(F32)
    out[...] = held[...].T.astype(BF16)


def near_kernel(starts, emit, neighbours, live, *refs):
    place = here()
    mine, theirs = refs[:5], refs[5 : 5 + (5 if starts[1] is not None else 1)]
    refs = refs[5 + len(theirs) :]
    blocks = refs[0]
    out_mine, out_theirs = refs[1], refs[2]
    image = refs[3] if emit else None
    held = refs[4]
    if not emit:
        source_blocks, blocks, arrived = blocks, refs[3], refs[5]
        copies = [
            pltpu.make_async_copy(source_blocks.at[n], blocks.at[n], arrived.at[n])
            for n in range(blocks.shape[0])
        ]
        for copy in copies:
            copy.start()
    spheres = out_mine.shape[0] // 2
    slots = blocks.shape[1]
    coeffs = blocks.shape[3]
    for j in range(5):
        for side in range(2):
            for r in range(2):
                rows = pl.ds(r * spheres, spheres)
                if side == 0:
                    value = mine[j][rows, pl.ds(0, 2 * coeffs)]
                elif starts[1] is not None:
                    value = theirs[j][rows, pl.ds(starts[1], 2 * coeffs)]
                else:
                    value = theirs[0][pl.ds((2 * j + r) * spheres, spheres), :]
                value = value.astype(F32)
                at = pl.ds(j * spheres, spheres)
                held[at, side * 2 + r, :] = value[:, :coeffs]
                held[at, 4 + side * 2 + r, :] = value[:, coeffs:]
    if emit:
        first = place[0] == 0
        for r in range(2):
            own = mine[0][pl.ds(r * spheres, spheres), :].astype(F32)
            other = theirs[0][pl.ds(r * spheres, spheres), :].astype(F32)
            image[:, r, :] = jnp.where(first, own, other).astype(BF16)
            image[:, 2 + r, :] = jnp.where(first, other, own).astype(BF16)

    for n in range(spheres):
        real = jnp.zeros((8, coeffs), F32)
        imag = jnp.zeros((8, coeffs), F32)
        if not emit:
            copies[n].wait()
        for k in range(slots):
            source = neighbours[n, k]
            chip = source // spheres
            near = jnp.where(chip // 4 == place[3] // 4, chip ^ place[3], 4)
            value = held[near * spheres + source % spheres]
            alive = place[0] * slots + k < live[n]
            value = jnp.where(alive, value, 0.0).astype(BF16)
            real += jnp.dot(value, blocks[n, k, 0], preferred_element_type=F32)
            imag += jnp.dot(value, blocks[n, k, 1], preferred_element_type=F32)
        near_re = real[:4] - imag[4:]
        near_im = imag[:4] + real[4:]
        for r in range(2):
            row = pl.ds(r * spheres + n, 1)
            out_mine[row, pl.ds(0, coeffs)] = near_re[r : r + 1]
            out_mine[row, pl.ds(coeffs, coeffs)] = near_im[r : r + 1]
            out_theirs[row, pl.ds(0, coeffs)] = near_re[2 + r : 3 + r]
            out_theirs[row, pl.ds(coeffs, coeffs)] = near_im[2 + r : 3 + r]


def near_call(starts, emit, neighbours, live, mine, theirs, blocks):
    spheres, slots, _, coeffs, _ = blocks.shape
    rows = 2 * spheres
    outs = [jax.ShapeDtypeStruct((rows, 2 * coeffs), F32)] * 2
    if emit:
        outs.append(jax.ShapeDtypeStruct((spheres, 4, 2 * coeffs), BF16))
    else:
        outs.append(pltpu.VMEM(blocks.shape, BF16))
    full = [VM] * (len(mine) + len(theirs))
    return pl.pallas_call(
        functools.partial(near_kernel, starts, emit),
        out_shape=tuple(outs),
        in_specs=[SM] * 2 + full + [VM if emit else HB],
        out_specs=(VM,) * len(outs),
        scratch_shapes=[pltpu.VMEM((5 * spheres, 8, coeffs), F32)]
        + ([] if emit else [pltpu.SemaphoreType.DMA((spheres,))]),
        cost_estimate=pl.CostEstimate(
            flops=2 * 8 * 2 * coeffs * coeffs * spheres * slots,
            bytes_accessed=blocks.size * 2,
            transcendentals=0,
        ),
        compiler_params=pltpu.CompilerParams(vmem_limit_bytes=(4 if emit else 34) << 20),
    )(neighbours, live, *mine, *theirs, blocks)


def far_kernel(
    box, list_mine, list_theirs, z0, z1, z2, z3, table_mine, table_theirs, turn, dis, out,
    source, factor, field, local
):
    place = here()
    own_boxes, listed = list_mine.shape
    boxes = 2 * own_boxes
    waves = source.shape[2]
    spheres = local.shape[1]
    first = place[0] == 0
    total = jnp.zeros((2 * boxes, 2 * waves), F32)
    for part in (z0, z1, z2, z3):
        total += part[:, pl.ds(0, 2 * waves)].astype(F32)
    for r in range(2):
        re = total[r * boxes : (r + 1) * boxes, :waves]
        im = total[r * boxes : (r + 1) * boxes, waves:]
        source[:, r, :] = re
        source[:, 2 + r, :] = im
        source[:, 4 + r, :] = -im
        source[:, 6 + r, :] = re
    size = table_mine.shape[0]
    mine, theirs = table_mine[...].astype(F32), table_theirs[...].astype(F32)
    factor[pl.ds(0, size), :] = jnp.where(first, mine, theirs)
    factor[pl.ds(size, size), :] = jnp.where(first, theirs, mine)
    upper = lax.broadcasted_iota(jnp.int32, (8, waves), 0) < 4

    def one_box(b, carry):
        row = b % own_boxes
        is_mine = b // own_boxes == place[0]
        sums = [jnp.zeros((8, waves), F32) for _ in range(2)]
        for f in range(listed):
            which = jnp.where(is_mine, list_mine[row, f], list_theirs[row, f])
            at = (b * listed + f) * 2
            weight = jnp.where(upper, factor[pl.ds(at, 1), :], factor[pl.ds(at + 1, 1), :])
            sums[f % 2] = sums[f % 2] + weight * source[which]
        both = sums[0] + sums[1]
        field[b] = both[:4] + both[4:]
        return carry

    lax.fori_loop(box[0], box[spheres - 1] + 1, one_box, 0)
    for n in range(spheres):
        local[:, n, :] = field[box[n]]
    re = local[pl.ds(0, 2)].reshape(2 * spheres, waves)
    im = local[pl.ds(2, 2)].reshape(2 * spheres, waves)
    cosine = turn[pl.ds(0, 2 * spheres), pl.ds(0, waves)]
    sine = turn[pl.ds(0, 2 * spheres), pl.ds(waves, waves)]
    shifted = jnp.concatenate([re * cosine + im * sine, im * cosine - re * sine], axis=1)
    dims = (((1,), (1,)), ((), ()))
    out[...] = lax.dot_general(shifted.astype(BF16), dis[...], dims, preferred_element_type=F32)


def scatter_kernel(far, near_mine, near_got, tmatrix, current, out):
    coeffs = tmatrix.shape[2]
    total = far[...] + (near_mine[...] + near_got[...])
    t_re = jnp.concatenate([tmatrix[:, 0], tmatrix[:, 0]], axis=0)
    t_im = jnp.concatenate([tmatrix[:, 1], tmatrix[:, 1]], axis=0)
    f_re, f_im = total[:, :coeffs], total[:, coeffs:]
    start = current[:, pl.ds(0, 2 * coeffs)].astype(F32)
    out[:, pl.ds(0, coeffs)] = (start[:, :coeffs] - (t_re * f_re - t_im * f_im)).astype(BF16)
    out[:, pl.ds(coeffs, coeffs)] = (start[:, coeffs:] - (t_re * f_im + t_im * f_re)).astype(BF16)


def join_kernel(mine, theirs, out):
    spheres = out.shape[0]
    first = lax.axis_index("far") == 0
    for r in range(2):
        own = mine[pl.ds(r * spheres, spheres), :].astype(F32)
        other = theirs[pl.ds(r * spheres, spheres), :].astype(F32)
        out[:, r, :] = jnp.where(first, own, other).astype(BF16)
        out[:, 2 + r, :] = jnp.where(first, other, own).astype(BF16)


def swap_far(block):
    return lax.ppermute(block, "far", [(0, 1), (1, 0)])


def kernel_shards(
    vectors, near_blocks, neighbours, live_counts, tmatrix, agg_matrix, sphere_box, agg_angle,
    far_list, far_factors, dis_matrix
):
    spheres, newton, width = vectors.shape
    own_boxes, listed = far_list.shape
    boxes = 2 * own_boxes
    waves = agg_matrix.shape[1] // 2
    rows = spheres * newton // 2
    entries = own_boxes * listed * 2
    later = (near_blocks, agg_matrix, neighbours, live_counts)
    message, edge = call(
        pack_kernel,
        [((rows, 1024 + waves + entries), BF16), ((rows, 1024), BF16)],
        [SM, VM, VM, VM] + [HB] * 4,
        (sphere_box, vectors, agg_angle, far_factors.reshape(entries, -1), *later),
        limit=60 << 20,
        held=True,
    )
    list_theirs = swap_far(far_list)
    current = message
    table = None
    for step in range(2):
        if step == 0:
            parts = xor_gather(message, (1, 2, 3))
            edge = edge_rows(edge)
            parts, edge, list_theirs = lax.optimization_barrier((parts, edge, list_theirs))
            block, turn, member, _ = call(
                functools.partial(first_waves_kernel, boxes),
                [
                    ((2 * boxes, 2 * waves + waves // 4 * entries // (2 * boxes)), BF16),
                    ((4 * rows, 2 * waves), F32),
                    ((4 * rows, 2 * boxes), BF16),
                    ((waves // 4, entries), F32),
                ],
                [VM] * 5,
                (*parts, agg_matrix),
            )
        else:
            parts = [current]
            for mask in (1, 2, 3):
                parts.append(swap_near(current, mask))
            edge = edge_rows(current)
            block, around = call(
                next_waves_kernel,
                [((2 * boxes, 2 * waves), BF16), ((5 * rows, width), BF16)],
                [VM] * 8,
                (*parts, edge, agg_matrix, turn, member),
            )
        pieces = xor_gather(block, (4, 8, 12))
        mine = (*parts, edge)
        if step == 0:
            near_mine, near_theirs, held_blocks = near_call(
                (0, 512), False, neighbours, live_counts, mine, mine, near_blocks
            )
        else:
            theirs = swap_far(around)
            near_mine, near_theirs, first_image = near_call(
                (0, None), True, neighbours, live_counts, mine, (theirs,), held_blocks
            )
        near_got = swap_far(near_theirs)
        if step == 0:
            pieces, near_mine = lax.optimization_barrier((pieces, near_mine))
            table = call(
                functools.partial(table_kernel, waves),
                [((entries, waves), BF16)],
                [VM] * 4,
                (*pieces,),
                [pltpu.VMEM((waves, entries), F32)],
            )[0]
            table = (table, swap_far(table))
        far_field = call(
            far_kernel,
            [((rows, width), F32)],
            [SM] * 3 + [VM] * 8,
            (
                sphere_box, far_list, list_theirs, *pieces, *table, turn, dis_matrix.T
            ),
            [
                pltpu.VMEM((boxes, 8, waves), F32),
                pltpu.VMEM((2 * entries, waves), F32),
                pltpu.VMEM((boxes, 4, waves), F32),
                pltpu.VMEM((4, spheres, waves), F32),
            ],
        )[0]
        current = call(
            scatter_kernel,
            [((rows, width), BF16)],
            [VM] * 5,
            (far_field, near_mine, near_got, tmatrix, current),
        )[0]
    second_image = call(
        join_kernel,
        [((spheres, newton, width), BF16)],
        [VM, VM],
        (current, swap_far(current)),
    )[0]
    return first_image, second_image


def shards(*args):
    if lax.axis_size("near") == 16 and lax.axis_size("far") == 2:
        return kernel_shards(*args)
    return plain_shards(*args)


def solution(mesh):
    return jax.shard_map(
        shards,
        mesh=mesh,
        in_specs=(
            P("near", None, None),
            P("near", "far", None, None, None),
            P("near", "far"),
            P("near"),
            P("near", None, None),
            P(),
            P("near"),
            P("near", None),
            P("far", None),
            P("far", None, None, "near"),
            P(),
        ),
        out_specs=(P("near", None, None), P("near", None, None)),
        check_vma=False,
    )
```

```python
import functools

import jax
import jax.numpy as jnp
from jax import lax
from jax.experimental import pallas as pl
from jax.experimental.pallas import tpu as pltpu
from jax.sharding import PartitionSpec as P

F32 = jnp.float32
BF16 = jnp.bfloat16
RADIX = 4


def complex_mul(left_re, left_im, right_re, right_im):
    return (left_re * right_re - left_im * right_im, left_re * right_im + left_im * right_re)


def swap_near(block, mask):
    count = lax.axis_size("near")
    return lax.ppermute(block, "near", [(i, i ^ mask) for i in range(count)])


def phase_masks():
    count = lax.axis_size("near")
    phases, step = [], 1
    while step < count:
        radix = min(RADIX, count // step)
        phases.append([step * j for j in range(1, radix)])
        step *= radix
    return phases


def xor_gather(block, masks):
    return [block] + [swap_near(block, mask) for mask in masks]


def in_order(parts, masks):
    step = masks[0]
    digit = lax.axis_index("near") // step % len(parts)
    stacked = jnp.stack(parts)
    return jnp.take(stacked, jnp.arange(len(parts)) ^ digit, axis=0)


def edge_rows(block):
    count = lax.axis_size("near")
    pairs = []
    for low in range(RADIX, count, RADIX):
        pairs.append((low - 1, low))
        pairs.append((low, low - 1))
    return lax.ppermute(block, "near", pairs) if pairs else jnp.zeros_like(block)


def edge_from_plane(diagonal):
    count = lax.axis_size("near")
    up = [(i, i + RADIX) for i in range(0, count - RADIX, RADIX)]
    down = [(i + RADIX, i) for i in range(RADIX - 1, count - RADIX, RADIX)]
    return lax.ppermute(diagonal, "near", up + down)


def over_far(block):
    count = lax.axis_size("far")
    if count == 2:
        other = lax.ppermute(block, "far", [(0, 1), (1, 0)])
        first = lax.axis_index("far") == 0
        return jnp.stack([jnp.where(first, block, other), jnp.where(first, other, block)])
    return lax.all_gather(block, "far", axis=0)


def near_share(partial, share):
    count = lax.axis_size("far")
    far_pos = lax.axis_index("far")
    mine = lax.dynamic_slice_in_dim(partial, far_pos % (partial.shape[1] // share) * share, share, 1)
    if count == 2:
        theirs = lax.dynamic_slice_in_dim(partial, (1 - far_pos) * share, share, 1)
        return mine + lax.ppermute(theirs, "far", [(0, 1), (1, 0)])
    total = lax.psum(partial, "far")
    return lax.dynamic_slice_in_dim(total, far_pos % (partial.shape[1] // share) * share, share, 1)


def plain_shards(
    vectors,
    near_blocks,
    neighbours,
    live_counts,
    tmatrix,
    agg_matrix,
    sphere_box,
    agg_angle,
    far_list,
    far_factors,
    dis_matrix,
):
    spheres, newton, width = vectors.shape
    coeffs = width // 2
    slots = neighbours.shape[1]
    far_count = lax.axis_size("far")
    own_boxes, listed = far_list.shape
    boxes = own_boxes * far_count
    waves = agg_matrix.shape[1] // 2
    share = newton // min(far_count, newton)
    splits = newton // share
    near_pos = lax.axis_index("near")
    far_pos = lax.axis_index("far")
    phases = phase_masks()
    rows = spheres * share

    def own_share(block):
        return lax.dynamic_slice_in_dim(block, far_pos % splits * share, share, 1)

    rounded = lax.reduce_precision(agg_angle, 8, 7)
    hi, low = rounded.astype(BF16), (agg_angle - rounded).astype(BF16)
    factors = far_factors.astype(BF16).reshape(-1, far_factors.shape[-1]).T
    lists = over_far_lists(far_list)
    extra = jnp.concatenate(
        [
            jnp.repeat(sphere_box, share).astype(BF16)[:, None],
            jnp.stack([hi, low]).reshape(rows, -1),
            factors.reshape(rows, -1),
        ],
        axis=1,
    )
    angle_width = 2 * spheres * waves // rows

    cosine = jnp.cos(agg_angle)
    sine = jnp.sin(agg_angle)
    alive = (far_pos * slots + jnp.arange(slots, dtype=jnp.int32))[None, :] < live_counts[:, None]
    chip = neighbours // spheres
    place = jnp.where(chip // RADIX == near_pos // RADIX, chip ^ near_pos, RADIX)
    local_index = place * spheres + neighbours % spheres

    state = {}
    images = []
    current = own_share(vectors)
    for step in range(2):
        flat = current.reshape(rows, width)
        edge = edge_rows(current)
        message = jnp.concatenate([flat, extra], axis=1) if step == 0 else flat
        parts = xor_gather(message, phases[0])
        group = len(parts)
        around = [p[:, :width].reshape(spheres, share, width) for p in parts]
        full = over_far(jnp.stack(around + [edge]))[:splits]
        full = jnp.moveaxis(full, 0, 2).reshape((group + 1) * spheres, newton, width)
        if step == 1:
            images.append(full[:spheres])
        if step == 0:
            box_ids = jnp.concatenate([p[:, width].reshape(spheres, share)[:, 0] for p in parts])
            angles = jnp.stack(
                [
                    p[:, width + 1 : width + 1 + angle_width].reshape(2, spheres, waves)
                    for p in parts
                ]
            ).astype(F32)
            angles = (angles[:, 0] + angles[:, 1]).reshape(group * spheres, waves)
            state["cos"], state["sin"] = jnp.cos(angles), jnp.sin(angles)
            state["member"] = (
                box_ids.astype(jnp.int32)[None, :] == jnp.arange(boxes, dtype=jnp.int32)[:, None]
            ).astype(F32)
            table = in_order([p[:, width + 1 + angle_width :] for p in parts], phases[0])
        product = jnp.dot(
            jnp.concatenate(around).reshape(group * rows, width),
            agg_matrix,
            preferred_element_type=F32,
        ).reshape(group * spheres, share, 2, waves)
        out_re, out_im = complex_mul(
            product[:, :, 0], product[:, :, 1], state["cos"][:, None], state["sin"][:, None]
        )
        stacked = jnp.concatenate([out_re, out_im], axis=-1)
        sums = jnp.einsum("bn,nrq->brq", state["member"], stacked, precision=lax.Precision.HIGHEST)
        for masks in phases[1:]:
            block = sums.astype(BF16).reshape(boxes * share, 2 * waves)
            if step == 0:
                block = jnp.concatenate([block, table.reshape(boxes * share, -1)], axis=1)
            pieces = xor_gather(block, masks)
            sums = sum(p[:, : 2 * waves].astype(F32) for p in pieces)
            sums = sums.reshape(boxes, share, 2 * waves)
            if step == 0:
                table = in_order([p[:, 2 * waves :] for p in pieces], masks)
        if step == 0:
            table = over_far(table.reshape(waves, own_boxes, listed, 2))
            table = table.transpose(0, 2, 3, 4, 1).reshape(boxes, listed, 2, waves)
            state["factors"] = table[sphere_box].astype(F32)
            state["sources"] = (
                lists[sphere_box][:, :, None] == jnp.arange(boxes, dtype=jnp.int32)
            ).astype(F32)
        gathered = jnp.where(alive[:, :, None, None], full[local_index], jnp.zeros((), BF16))
        both = jnp.concatenate([gathered[..., :coeffs], gathered[..., coeffs:]], axis=2)
        with_real = jnp.einsum(
            "nkrc,nkcd->nrd", both, near_blocks[:, :, 0], preferred_element_type=F32
        )
        with_imag = jnp.einsum(
            "nkrc,nkcd->nrd", both, near_blocks[:, :, 1], preferred_element_type=F32
        )
        near_re = with_real[:, :newton] - with_imag[:, newton:]
        near_im = with_imag[:, :newton] + with_real[:, newton:]
        near_field = near_share(jnp.concatenate([near_re, near_im], axis=-1), share)
        picked = jnp.einsum(
            "nfb,brq->nfrq", state["sources"], sums, precision=lax.Precision.HIGHEST
        )
        fac = state["factors"]
        in_re, in_im = complex_mul(
            fac[:, :, None, 0], fac[:, :, None, 1], picked[..., :waves], picked[..., waves:]
        )
        in_re, in_im = jnp.sum(in_re, axis=1), jnp.sum(in_im, axis=1)
        local_re, local_im = complex_mul(in_re, in_im, cosine[:, None], -sine[:, None])
        local_waves = jnp.concatenate([local_re, local_im], axis=-1).astype(BF16)
        far_field = jnp.dot(
            local_waves.reshape(rows, 2 * waves), dis_matrix, preferred_element_type=F32
        ).reshape(spheres, share, width)
        field = near_field + far_field
        scat_re, scat_im = complex_mul(
            tmatrix[:, None, 0], tmatrix[:, None, 1], field[..., :coeffs], field[..., coeffs:]
        )
        current = (current.astype(F32) - jnp.concatenate([scat_re, scat_im], axis=-1)).astype(BF16)
    last = over_far(current)[:splits]
    images.append(jnp.moveaxis(last, 0, 1).reshape(spheres, newton, width))
    return tuple(images)


def over_far_lists(far_list):
    gathered = over_far(far_list)
    return gathered.reshape(-1, far_list.shape[1])


VM = pl.BlockSpec(memory_space=pltpu.VMEM)
SM = pl.BlockSpec(memory_space=pltpu.SMEM)
HB = pl.BlockSpec(memory_space=pl.ANY)


def call(kernel, outs, specs, args, scratch=(), flops=0, moved=6 << 20, limit=4 << 20, held=False):
    make = pltpu.VMEM if held else jax.ShapeDtypeStruct
    return pl.pallas_call(
        kernel,
        out_shape=tuple(make(shape, kind) for shape, kind in outs),
        in_specs=list(specs),
        out_specs=(VM,) * len(outs),
        scratch_shapes=list(scratch),
        cost_estimate=pl.CostEstimate(flops=flops, bytes_accessed=moved, transcendentals=0),
        compiler_params=pltpu.CompilerParams(vmem_limit_bytes=limit),
    )(*args)


def here():
    near_pos = lax.axis_index("near")
    return lax.axis_index("far"), near_pos % 4, near_pos // 4, near_pos


def pack_kernel(box, vectors, angle, factors, *refs):
    out = refs[-1]
    place = here()
    spheres, newton, width = vectors.shape
    share = newton // 2
    waves = angle.shape[1]
    first = place[0] == 0
    values = vectors[...].astype(F32)
    for r in range(share):
        low, high = values[:, r], values[:, share + r]
        rows = pl.ds(r * spheres, spheres)
        out[rows, pl.ds(0, width)] = jnp.where(first, low, high).astype(BF16)
        out[rows, pl.ds(512, width)] = jnp.where(first, high, low).astype(BF16)
    lane = lax.broadcasted_iota(jnp.int32, (spheres * share, 512 - width), 0) % spheres
    ids = jnp.zeros((spheres * share, 512 - width), F32)
    for n in range(spheres):
        ids = jnp.where(lane == n, box[n].astype(F32), ids)
    out[:, pl.ds(width, 512 - width)] = ids.astype(BF16)
    hi = angle[...].astype(BF16)
    low = (angle[...] - hi.astype(F32)).astype(BF16)
    out[pl.ds(0, spheres), pl.ds(1024, waves)] = hi
    out[pl.ds(spheres, spheres), pl.ds(1024, waves)] = low
    out[:, pl.ds(1024 + waves, factors.shape[0])] = factors[...].T.astype(BF16)


def sum_rows(member, waves):
    dims = (((0,), (0,)), ((), ()))
    hi = waves.astype(BF16)
    low = (waves - hi.astype(F32)).astype(BF16)
    return lax.dot_general(member, hi, dims, preferred_element_type=F32) + lax.dot_general(
        member, low, dims, preferred_element_type=F32
    )


def turned(product, turn, waves):
    cosine, sine = turn[:, :waves], turn[:, waves:]
    re, im = product[:, :waves], product[:, waves:]
    return jnp.concatenate([re * cosine - im * sine, re * sine + im * cosine], axis=1)


def first_waves_kernel(boxes, p0, p1, p2, p3, agg, out, turn, member, table):
    place = here()
    parts = (p0, p1, p2, p3)
    width = agg.shape[0]
    waves = agg.shape[1] // 2
    rows = p0.shape[0]
    half = rows // 2
    held = table.shape[0] // 4
    for j, part in enumerate(parts):
        angle = part[pl.ds(0, half), pl.ds(1024, waves)].astype(F32)
        angle += part[pl.ds(half, half), pl.ds(1024, waves)].astype(F32)
        both = jnp.concatenate([jnp.cos(angle), jnp.sin(angle)], axis=1)
        turn[pl.ds(j * rows, half), :] = both
        turn[pl.ds(j * rows + half, half), :] = both
        ids = part[:, pl.ds(width, 1)].astype(F32)
        row = lax.broadcasted_iota(jnp.int32, (rows, 2 * boxes), 0) // half
        col = lax.broadcasted_iota(jnp.int32, (rows, 2 * boxes), 1)
        hit = (ids == (col % boxes).astype(F32)) & (row == col // boxes)
        member[pl.ds(j * rows, rows), :] = jnp.where(hit, 1.0, 0.0).astype(BF16)
        at = pl.multiple_of((place[1] ^ j) * held, held)
        table[pl.ds(at, held), :] = part[:, pl.ds(1024 + waves, table.shape[1])].astype(F32)
    flat = jnp.concatenate([p[:, pl.ds(0, width)] for p in parts], axis=0)
    product = jnp.dot(flat, agg[...], preferred_element_type=F32)
    sums = sum_rows(member[...], turned(product, turn[...], waves))
    out[:, pl.ds(0, 2 * waves)] = sums.astype(BF16)
    lines = out.shape[0]
    span = table.shape[1]
    for j in range(table.shape[0] // lines):
        out[:, pl.ds(2 * waves + j * span, span)] = table[pl.ds(j * lines, lines), :].astype(BF16)


def next_waves_kernel(p0, p1, p2, p3, agg, turn, member, out, around):
    waves = agg.shape[1] // 2
    rows = p0.shape[0]
    for j, part in enumerate((p0, p1, p2, p3)):
        around[pl.ds(j * rows, rows), :] = part[...]
    flat = jnp.concatenate([p0[...], p1[...], p2[...], p3[...]], axis=0)
    product = jnp.dot(flat, agg[...], preferred_element_type=F32)
    out[...] = sum_rows(member[...], turned(product, turn[...], waves)).astype(BF16)


def table_kernel(waves, z0, z1, z2, z3, out, held):
    place = here()
    lines = z0.shape[0]
    span = held.shape[1]
    pieces = (z0.shape[1] - 2 * waves) // span
    for j, part in enumerate((z0, z1, z2, z3)):
        for i in range(pieces):
            at = pl.multiple_of(((place[2] ^ j) * pieces + i) * lines, lines)
            held[pl.ds(at, lines), :] = part[:, pl.ds(2 * waves + i * span, span)].astype(F32)
    out[...] = held[...].T.astype(BF16)


def near_kernel(starts, emit, neighbours, live, *refs):
    place = here()
    mine, theirs = refs[:5], refs[5 : 5 + (5 if starts[1] is not None else 2)]
    refs = refs[5 + len(theirs) :]
    blocks = refs[0]
    out_mine, out_theirs = refs[1], refs[2]
    image = refs[3] if emit else None
    held = refs[4]
    if not emit:
        source_blocks, blocks, arrived = blocks, refs[3], refs[5]
        copies = [
            pltpu.make_async_copy(source_blocks.at[n], blocks.at[n], arrived.at[n])
            for n in range(blocks.shape[0])
        ]
        for copy in copies:
            copy.start()
    spheres = out_mine.shape[0] // 2
    slots = blocks.shape[1]
    coeffs = blocks.shape[3]
    for j in range(5):
        for side in range(2):
            for r in range(2):
                rows = pl.ds(r * spheres, spheres)
                if side == 0:
                    value = mine[j][rows, pl.ds(0, 2 * coeffs)]
                elif starts[1] is not None:
                    value = theirs[j][rows, pl.ds(starts[1], 2 * coeffs)]
                else:
                    value = theirs[j // 4][pl.ds((2 * (j % 4) + r) * spheres, spheres), :]
                value = value.astype(F32)
                at = pl.ds(j * spheres, spheres)
                held[at, side * 2 + r, :] = value[:, :coeffs]
                held[at, 4 + side * 2 + r, :] = value[:, coeffs:]
    if emit:
        first = place[0] == 0
        for r in range(2):
            own = mine[0][pl.ds(r * spheres, spheres), :].astype(F32)
            other = theirs[0][pl.ds(r * spheres, spheres), :].astype(F32)
            image[:, r, :] = jnp.where(first, own, other).astype(BF16)
            image[:, 2 + r, :] = jnp.where(first, other, own).astype(BF16)

    for n in range(spheres):
        real = jnp.zeros((8, coeffs), F32)
        imag = jnp.zeros((8, coeffs), F32)
        if not emit:
            copies[n].wait()
        for k in range(slots):
            source = neighbours[n, k]
            chip = source // spheres
            near = jnp.where(chip // 4 == place[3] // 4, chip ^ place[3], 4)
            value = held[near * spheres + source % spheres]
            alive = place[0] * slots + k < live[n]
            value = jnp.where(alive, value, 0.0).astype(BF16)
            real += jnp.dot(value, blocks[n, k, 0], preferred_element_type=F32)
            imag += jnp.dot(value, blocks[n, k, 1], preferred_element_type=F32)
        near_re = real[:4] - imag[4:]
        near_im = imag[:4] + real[4:]
        for r in range(2):
            row = pl.ds(r * spheres + n, 1)
            out_mine[row, pl.ds(0, coeffs)] = near_re[r : r + 1]
            out_mine[row, pl.ds(coeffs, coeffs)] = near_im[r : r + 1]
            out_theirs[row, pl.ds(0, coeffs)] = near_re[2 + r : 3 + r]
            out_theirs[row, pl.ds(coeffs, coeffs)] = near_im[2 + r : 3 + r]


def near_call(starts, emit, neighbours, live, mine, theirs, blocks):
    spheres, slots, _, coeffs, _ = blocks.shape
    rows = 2 * spheres
    outs = [jax.ShapeDtypeStruct((rows, 2 * coeffs), F32)] * 2
    if emit:
        outs.append(jax.ShapeDtypeStruct((spheres, 4, 2 * coeffs), BF16))
    else:
        outs.append(pltpu.VMEM(blocks.shape, BF16))
    full = [VM] * (len(mine) + len(theirs))
    return pl.pallas_call(
        functools.partial(near_kernel, starts, emit),
        out_shape=tuple(outs),
        in_specs=[SM] * 2 + full + [VM if emit else HB],
        out_specs=(VM,) * len(outs),
        scratch_shapes=[pltpu.VMEM((5 * spheres, 8, coeffs), F32)]
        + ([] if emit else [pltpu.SemaphoreType.DMA((spheres,))]),
        cost_estimate=pl.CostEstimate(
            flops=2 * 8 * 2 * coeffs * coeffs * spheres * slots,
            bytes_accessed=blocks.size * 2,
            transcendentals=0,
        ),
        compiler_params=pltpu.CompilerParams(vmem_limit_bytes=(4 if emit else 34) << 20),
    )(neighbours, live, *mine, *theirs, blocks)


def far_kernel(
    box, list_mine, list_theirs, z0, z1, z2, z3, table_mine, table_theirs, turn, dis, out,
    source, factor, field, local
):
    place = here()
    own_boxes, listed = list_mine.shape
    boxes = 2 * own_boxes
    waves = source.shape[2]
    spheres = local.shape[1]
    first = place[0] == 0
    total = jnp.zeros((2 * boxes, 2 * waves), F32)
    for part in (z0, z1, z2, z3):
        total += part[:, pl.ds(0, 2 * waves)].astype(F32)
    for r in range(2):
        re = total[r * boxes : (r + 1) * boxes, :waves]
        im = total[r * boxes : (r + 1) * boxes, waves:]
        source[:, r, :] = re
        source[:, 2 + r, :] = im
        source[:, 4 + r, :] = -im
        source[:, 6 + r, :] = re
    size = table_mine.shape[0]
    mine, theirs = table_mine[...].astype(F32), table_theirs[...].astype(F32)
    factor[pl.ds(0, size), :] = jnp.where(first, mine, theirs)
    factor[pl.ds(size, size), :] = jnp.where(first, theirs, mine)
    upper = lax.broadcasted_iota(jnp.int32, (8, waves), 0) < 4

    def one_box(b, carry):
        row = b % own_boxes
        is_mine = b // own_boxes == place[0]
        sums = [jnp.zeros((8, waves), F32) for _ in range(2)]
        for f in range(listed):
            which = jnp.where(is_mine, list_mine[row, f], list_theirs[row, f])
            at = (b * listed + f) * 2
            weight = jnp.where(upper, factor[pl.ds(at, 1), :], factor[pl.ds(at + 1, 1), :])
            sums[f % 2] = sums[f % 2] + weight * source[which]
        both = sums[0] + sums[1]
        field[b] = both[:4] + both[4:]
        return carry

    lax.fori_loop(box[0], box[spheres - 1] + 1, one_box, 0)
    for n in range(spheres):
        local[:, n, :] = field[box[n]]
    re = local[pl.ds(0, 2)].reshape(2 * spheres, waves)
    im = local[pl.ds(2, 2)].reshape(2 * spheres, waves)
    cosine = turn[pl.ds(0, 2 * spheres), pl.ds(0, waves)]
    sine = turn[pl.ds(0, 2 * spheres), pl.ds(waves, waves)]
    shifted = jnp.concatenate([re * cosine + im * sine, im * cosine - re * sine], axis=1)
    dims = (((1,), (1,)), ((), ()))
    out[...] = lax.dot_general(shifted.astype(BF16), dis[...], dims, preferred_element_type=F32)


def scatter_kernel(far, near_mine, near_got, tmatrix, current, out):
    coeffs = tmatrix.shape[2]
    total = far[...] + (near_mine[...] + near_got[...])
    t_re = jnp.concatenate([tmatrix[:, 0], tmatrix[:, 0]], axis=0)
    t_im = jnp.concatenate([tmatrix[:, 1], tmatrix[:, 1]], axis=0)
    f_re, f_im = total[:, :coeffs], total[:, coeffs:]
    start = current[:, pl.ds(0, 2 * coeffs)].astype(F32)
    out[:, pl.ds(0, coeffs)] = (start[:, :coeffs] - (t_re * f_re - t_im * f_im)).astype(BF16)
    out[:, pl.ds(coeffs, coeffs)] = (start[:, coeffs:] - (t_re * f_im + t_im * f_re)).astype(BF16)


def join_kernel(mine, theirs, out):
    spheres = out.shape[0]
    first = lax.axis_index("far") == 0
    for r in range(2):
        own = mine[pl.ds(r * spheres, spheres), :].astype(F32)
        other = theirs[pl.ds(r * spheres, spheres), :].astype(F32)
        out[:, r, :] = jnp.where(first, own, other).astype(BF16)
        out[:, 2 + r, :] = jnp.where(first, other, own).astype(BF16)


def swap_far(block):
    return lax.ppermute(block, "far", [(0, 1), (1, 0)])


def kernel_shards(
    vectors, near_blocks, neighbours, live_counts, tmatrix, agg_matrix, sphere_box, agg_angle,
    far_list, far_factors, dis_matrix
):
    spheres, newton, width = vectors.shape
    own_boxes, listed = far_list.shape
    boxes = 2 * own_boxes
    waves = agg_matrix.shape[1] // 2
    rows = spheres * newton // 2
    entries = own_boxes * listed * 2
    later = (near_blocks, agg_matrix, neighbours, live_counts)
    message = call(
        pack_kernel,
        [((rows, 1024 + waves + entries), BF16)],
        [SM, VM, VM, VM] + [HB] * 4,
        (sphere_box, vectors, agg_angle, far_factors.reshape(entries, -1), *later),
        limit=60 << 20,
        held=True,
    )[0]
    list_theirs = swap_far(far_list)
    current = message
    table = None
    for step in range(2):
        if step == 0:
            parts = xor_gather(message, (1, 2, 3))
            parts, list_theirs = lax.optimization_barrier((parts, list_theirs))
            block, turn, member, _ = call(
                functools.partial(first_waves_kernel, boxes),
                [
                    ((2 * boxes, 2 * waves + waves // 4 * entries // (2 * boxes)), BF16),
                    ((4 * rows, 2 * waves), F32),
                    ((4 * rows, 2 * boxes), BF16),
                    ((waves // 4, entries), F32),
                ],
                [VM] * 5,
                (*parts, agg_matrix),
            )
        else:
            parts = xor_gather(current, (1, 2, 3))
            block, around = call(
                next_waves_kernel,
                [((2 * boxes, 2 * waves), BF16), ((4 * rows, width), BF16)],
                [VM] * 7,
                (*parts, agg_matrix, turn, member),
            )
        edge = edge_from_plane(parts[3])
        pieces = [block]
        for mask in (4, 8, 12):
            pieces.append(swap_near(block, mask))
        mine = (*parts, edge)
        if step == 0:
            near_mine, near_theirs, held_blocks = near_call(
                (0, 512), False, neighbours, live_counts, mine, mine, near_blocks
            )
        else:
            around = swap_far(around)
            theirs = (around, swap_far(edge))
            near_mine, near_theirs, first_image = near_call(
                (0, None), True, neighbours, live_counts, mine, theirs, held_blocks
            )
        near_got = swap_far(near_theirs)
        if step == 0:
            pieces, near_mine = lax.optimization_barrier((pieces, near_mine))
            table = call(
                functools.partial(table_kernel, waves),
                [((entries, waves), BF16)],
                [VM] * 4,
                (*pieces,),
                [pltpu.VMEM((waves, entries), F32)],
            )[0]
            table = (table, swap_far(table))
        far_field = call(
            far_kernel,
            [((rows, width), F32)],
            [SM] * 3 + [VM] * 8,
            (
                sphere_box, far_list, list_theirs, *pieces, *table, turn, dis_matrix.T
            ),
            [
                pltpu.VMEM((boxes, 8, waves), F32),
                pltpu.VMEM((2 * entries, waves), F32),
                pltpu.VMEM((boxes, 4, waves), F32),
                pltpu.VMEM((4, spheres, waves), F32),
            ],
        )[0]
        current = call(
            scatter_kernel,
            [((rows, width), BF16)],
            [VM] * 5,
            (far_field, near_mine, near_got, tmatrix, current),
        )[0]
    second_image = call(
        join_kernel,
        [((spheres, newton, width), BF16)],
        [VM, VM],
        (current, swap_far(current)),
    )[0]
    return first_image, second_image


def shards(*args):
    if lax.axis_size("near") == 16 and lax.axis_size("far") == 2:
        return kernel_shards(*args)
    return plain_shards(*args)


def solution(mesh):
    return jax.shard_map(
        shards,
        mesh=mesh,
        in_specs=(
            P("near", None, None),
            P("near", "far", None, None, None),
            P("near", "far"),
            P("near"),
            P("near", None, None),
            P(),
            P("near"),
            P("near", None),
            P("far", None),
            P("far", None, None, "near"),
            P(),
        ),
        out_specs=(P("near", None, None), P("near", None, None)),
        check_vma=False,
    )
```

```python
import functools

import jax
import jax.numpy as jnp
from jax import lax
from jax.experimental import pallas as pl
from jax.experimental.pallas import tpu as pltpu
from jax.sharding import PartitionSpec as P

F32 = jnp.float32
BF16 = jnp.bfloat16
RADIX = 4


def complex_mul(left_re, left_im, right_re, right_im):
    return (left_re * right_re - left_im * right_im, left_re * right_im + left_im * right_re)


def swap_near(block, mask):
    count = lax.axis_size("near")
    return lax.ppermute(block, "near", [(i, i ^ mask) for i in range(count)])


def phase_masks():
    count = lax.axis_size("near")
    phases, step = [], 1
    while step < count:
        radix = min(RADIX, count // step)
        phases.append([step * j for j in range(1, radix)])
        step *= radix
    return phases


def xor_gather(block, masks):
    return [block] + [swap_near(block, mask) for mask in masks]


def in_order(parts, masks):
    step = masks[0]
    digit = lax.axis_index("near") // step % len(parts)
    stacked = jnp.stack(parts)
    return jnp.take(stacked, jnp.arange(len(parts)) ^ digit, axis=0)


def edge_rows(block):
    count = lax.axis_size("near")
    pairs = []
    for low in range(RADIX, count, RADIX):
        pairs.append((low - 1, low))
        pairs.append((low, low - 1))
    return lax.ppermute(block, "near", pairs) if pairs else jnp.zeros_like(block)


def edge_pairs():
    count = lax.axis_size("near")
    up = [(i, i + RADIX) for i in range(0, count - RADIX, RADIX)]
    down = [(i + RADIX, i) for i in range(RADIX - 1, count - RADIX, RADIX)]
    return up + down


def edge_from_plane(diagonal):
    return lax.ppermute(diagonal, "near", edge_pairs())


def edge_of_second_core(diagonal):
    pairs = [(2 * source + 1, 2 * target + 1) for source, target in edge_pairs()]
    return lax.ppermute(diagonal, ("near", "far"), pairs)


def edge_to_first_core(edge):
    ends = sorted(target for _, target in edge_pairs())
    return lax.ppermute(edge, ("near", "far"), [(2 * i + 1, 2 * i) for i in ends])


def over_far(block):
    count = lax.axis_size("far")
    if count == 2:
        other = lax.ppermute(block, "far", [(0, 1), (1, 0)])
        first = lax.axis_index("far") == 0
        return jnp.stack([jnp.where(first, block, other), jnp.where(first, other, block)])
    return lax.all_gather(block, "far", axis=0)


def near_share(partial, share):
    count = lax.axis_size("far")
    far_pos = lax.axis_index("far")
    mine = lax.dynamic_slice_in_dim(partial, far_pos % (partial.shape[1] // share) * share, share, 1)
    if count == 2:
        theirs = lax.dynamic_slice_in_dim(partial, (1 - far_pos) * share, share, 1)
        return mine + lax.ppermute(theirs, "far", [(0, 1), (1, 0)])
    total = lax.psum(partial, "far")
    return lax.dynamic_slice_in_dim(total, far_pos % (partial.shape[1] // share) * share, share, 1)


def plain_shards(
    vectors,
    near_blocks,
    neighbours,
    live_counts,
    tmatrix,
    agg_matrix,
    sphere_box,
    agg_angle,
    far_list,
    far_factors,
    dis_matrix,
):
    spheres, newton, width = vectors.shape
    coeffs = width // 2
    slots = neighbours.shape[1]
    far_count = lax.axis_size("far")
    own_boxes, listed = far_list.shape
    boxes = own_boxes * far_count
    waves = agg_matrix.shape[1] // 2
    share = newton // min(far_count, newton)
    splits = newton // share
    near_pos = lax.axis_index("near")
    far_pos = lax.axis_index("far")
    phases = phase_masks()
    rows = spheres * share

    def own_share(block):
        return lax.dynamic_slice_in_dim(block, far_pos % splits * share, share, 1)

    rounded = lax.reduce_precision(agg_angle, 8, 7)
    hi, low = rounded.astype(BF16), (agg_angle - rounded).astype(BF16)
    factors = far_factors.astype(BF16).reshape(-1, far_factors.shape[-1]).T
    lists = over_far_lists(far_list)
    extra = jnp.concatenate(
        [
            jnp.repeat(sphere_box, share).astype(BF16)[:, None],
            jnp.stack([hi, low]).reshape(rows, -1),
            factors.reshape(rows, -1),
        ],
        axis=1,
    )
    angle_width = 2 * spheres * waves // rows

    cosine = jnp.cos(agg_angle)
    sine = jnp.sin(agg_angle)
    alive = (far_pos * slots + jnp.arange(slots, dtype=jnp.int32))[None, :] < live_counts[:, None]
    chip = neighbours // spheres
    place = jnp.where(chip // RADIX == near_pos // RADIX, chip ^ near_pos, RADIX)
    local_index = place * spheres + neighbours % spheres

    state = {}
    images = []
    current = own_share(vectors)
    for step in range(2):
        flat = current.reshape(rows, width)
        edge = edge_rows(current)
        message = jnp.concatenate([flat, extra], axis=1) if step == 0 else flat
        parts = xor_gather(message, phases[0])
        group = len(parts)
        around = [p[:, :width].reshape(spheres, share, width) for p in parts]
        full = over_far(jnp.stack(around + [edge]))[:splits]
        full = jnp.moveaxis(full, 0, 2).reshape((group + 1) * spheres, newton, width)
        if step == 1:
            images.append(full[:spheres])
        if step == 0:
            box_ids = jnp.concatenate([p[:, width].reshape(spheres, share)[:, 0] for p in parts])
            angles = jnp.stack(
                [
                    p[:, width + 1 : width + 1 + angle_width].reshape(2, spheres, waves)
                    for p in parts
                ]
            ).astype(F32)
            angles = (angles[:, 0] + angles[:, 1]).reshape(group * spheres, waves)
            state["cos"], state["sin"] = jnp.cos(angles), jnp.sin(angles)
            state["member"] = (
                box_ids.astype(jnp.int32)[None, :] == jnp.arange(boxes, dtype=jnp.int32)[:, None]
            ).astype(F32)
            table = in_order([p[:, width + 1 + angle_width :] for p in parts], phases[0])
        product = jnp.dot(
            jnp.concatenate(around).reshape(group * rows, width),
            agg_matrix,
            preferred_element_type=F32,
        ).reshape(group * spheres, share, 2, waves)
        out_re, out_im = complex_mul(
            product[:, :, 0], product[:, :, 1], state["cos"][:, None], state["sin"][:, None]
        )
        stacked = jnp.concatenate([out_re, out_im], axis=-1)
        sums = jnp.einsum("bn,nrq->brq", state["member"], stacked, precision=lax.Precision.HIGHEST)
        for masks in phases[1:]:
            block = sums.astype(BF16).reshape(boxes * share, 2 * waves)
            if step == 0:
                block = jnp.concatenate([block, table.reshape(boxes * share, -1)], axis=1)
            pieces = xor_gather(block, masks)
            sums = sum(p[:, : 2 * waves].astype(F32) for p in pieces)
            sums = sums.reshape(boxes, share, 2 * waves)
            if step == 0:
                table = in_order([p[:, 2 * waves :] for p in pieces], masks)
        if step == 0:
            table = over_far(table.reshape(waves, own_boxes, listed, 2))
            table = table.transpose(0, 2, 3, 4, 1).reshape(boxes, listed, 2, waves)
            state["factors"] = table[sphere_box].astype(F32)
            state["sources"] = (
                lists[sphere_box][:, :, None] == jnp.arange(boxes, dtype=jnp.int32)
            ).astype(F32)
        gathered = jnp.where(alive[:, :, None, None], full[local_index], jnp.zeros((), BF16))
        both = jnp.concatenate([gathered[..., :coeffs], gathered[..., coeffs:]], axis=2)
        with_real = jnp.einsum(
            "nkrc,nkcd->nrd", both, near_blocks[:, :, 0], preferred_element_type=F32
        )
        with_imag = jnp.einsum(
            "nkrc,nkcd->nrd", both, near_blocks[:, :, 1], preferred_element_type=F32
        )
        near_re = with_real[:, :newton] - with_imag[:, newton:]
        near_im = with_imag[:, :newton] + with_real[:, newton:]
        near_field = near_share(jnp.concatenate([near_re, near_im], axis=-1), share)
        picked = jnp.einsum(
            "nfb,brq->nfrq", state["sources"], sums, precision=lax.Precision.HIGHEST
        )
        fac = state["factors"]
        in_re, in_im = complex_mul(
            fac[:, :, None, 0], fac[:, :, None, 1], picked[..., :waves], picked[..., waves:]
        )
        in_re, in_im = jnp.sum(in_re, axis=1), jnp.sum(in_im, axis=1)
        local_re, local_im = complex_mul(in_re, in_im, cosine[:, None], -sine[:, None])
        local_waves = jnp.concatenate([local_re, local_im], axis=-1).astype(BF16)
        far_field = jnp.dot(
            local_waves.reshape(rows, 2 * waves), dis_matrix, preferred_element_type=F32
        ).reshape(spheres, share, width)
        field = near_field + far_field
        scat_re, scat_im = complex_mul(
            tmatrix[:, None, 0], tmatrix[:, None, 1], field[..., :coeffs], field[..., coeffs:]
        )
        current = (current.astype(F32) - jnp.concatenate([scat_re, scat_im], axis=-1)).astype(BF16)
    last = over_far(current)[:splits]
    images.append(jnp.moveaxis(last, 0, 1).reshape(spheres, newton, width))
    return tuple(images)


def over_far_lists(far_list):
    gathered = over_far(far_list)
    return gathered.reshape(-1, far_list.shape[1])


VM = pl.BlockSpec(memory_space=pltpu.VMEM)
SM = pl.BlockSpec(memory_space=pltpu.SMEM)
HB = pl.BlockSpec(memory_space=pl.ANY)


def call(kernel, outs, specs, args, scratch=(), flops=0, moved=6 << 20, limit=4 << 20, held=False):
    make = pltpu.VMEM if held else jax.ShapeDtypeStruct
    return pl.pallas_call(
        kernel,
        out_shape=tuple(make(shape, kind) for shape, kind in outs),
        in_specs=list(specs),
        out_specs=(VM,) * len(outs),
        scratch_shapes=list(scratch),
        cost_estimate=pl.CostEstimate(flops=flops, bytes_accessed=moved, transcendentals=0),
        compiler_params=pltpu.CompilerParams(vmem_limit_bytes=limit),
    )(*args)


def here():
    near_pos = lax.axis_index("near")
    return lax.axis_index("far"), near_pos % 4, near_pos // 4, near_pos


def pack_kernel(box, vectors, angle, factors, *refs):
    out = refs[-1]
    place = here()
    spheres, newton, width = vectors.shape
    share = newton // 2
    waves = angle.shape[1]
    first = place[0] == 0
    values = vectors[...].astype(F32)
    for r in range(share):
        low, high = values[:, r], values[:, share + r]
        rows = pl.ds(r * spheres, spheres)
        out[rows, pl.ds(0, width)] = jnp.where(first, low, high).astype(BF16)
        out[rows, pl.ds(512, width)] = jnp.where(first, high, low).astype(BF16)
    lane = lax.broadcasted_iota(jnp.int32, (spheres * share, 512 - width), 0) % spheres
    ids = jnp.zeros((spheres * share, 512 - width), F32)
    for n in range(spheres):
        ids = jnp.where(lane == n, box[n].astype(F32), ids)
    out[:, pl.ds(width, 512 - width)] = ids.astype(BF16)
    hi = angle[...].astype(BF16)
    low = (angle[...] - hi.astype(F32)).astype(BF16)
    out[pl.ds(0, spheres), pl.ds(1024, waves)] = hi
    out[pl.ds(spheres, spheres), pl.ds(1024, waves)] = low
    out[:, pl.ds(1024 + waves, factors.shape[0])] = factors[...].T.astype(BF16)


def sum_rows(member, waves):
    dims = (((0,), (0,)), ((), ()))
    hi = waves.astype(BF16)
    low = (waves - hi.astype(F32)).astype(BF16)
    return lax.dot_general(member, hi, dims, preferred_element_type=F32) + lax.dot_general(
        member, low, dims, preferred_element_type=F32
    )


def turned(product, turn, waves):
    cosine, sine = turn[:, :waves], turn[:, waves:]
    re, im = product[:, :waves], product[:, waves:]
    return jnp.concatenate([re * cosine - im * sine, re * sine + im * cosine], axis=1)


def first_waves_kernel(boxes, p0, p1, p2, p3, agg, out, turn, member, table):
    place = here()
    parts = (p0, p1, p2, p3)
    width = agg.shape[0]
    waves = agg.shape[1] // 2
    rows = p0.shape[0]
    half = rows // 2
    held = table.shape[0] // 4
    for j, part in enumerate(parts):
        angle = part[pl.ds(0, half), pl.ds(1024, waves)].astype(F32)
        angle += part[pl.ds(half, half), pl.ds(1024, waves)].astype(F32)
        both = jnp.concatenate([jnp.cos(angle), jnp.sin(angle)], axis=1)
        turn[pl.ds(j * rows, half), :] = both
        turn[pl.ds(j * rows + half, half), :] = both
        ids = part[:, pl.ds(width, 1)].astype(F32)
        row = lax.broadcasted_iota(jnp.int32, (rows, 2 * boxes), 0) // half
        col = lax.broadcasted_iota(jnp.int32, (rows, 2 * boxes), 1)
        hit = (ids == (col % boxes).astype(F32)) & (row == col // boxes)
        member[pl.ds(j * rows, rows), :] = jnp.where(hit, 1.0, 0.0).astype(BF16)
        at = pl.multiple_of((place[1] ^ j) * held, held)
        table[pl.ds(at, held), :] = part[:, pl.ds(1024 + waves, table.shape[1])].astype(F32)
    flat = jnp.concatenate([p[:, pl.ds(0, width)] for p in parts], axis=0)
    product = jnp.dot(flat, agg[...], preferred_element_type=F32)
    sums = sum_rows(member[...], turned(product, turn[...], waves))
    out[:, pl.ds(0, 2 * waves)] = sums.astype(BF16)
    lines = out.shape[0]
    span = table.shape[1]
    for j in range(table.shape[0] // lines):
        out[:, pl.ds(2 * waves + j * span, span)] = table[pl.ds(j * lines, lines), :].astype(BF16)


def next_waves_kernel(p0, p1, p2, p3, agg, turn, member, out, around):
    waves = agg.shape[1] // 2
    rows = p0.shape[0]
    for j, part in enumerate((p0, p1, p2, p3)):
        around[pl.ds(j * rows, rows), :] = part[...]
    flat = jnp.concatenate([p0[...], p1[...], p2[...], p3[...]], axis=0)
    product = jnp.dot(flat, agg[...], preferred_element_type=F32)
    out[...] = sum_rows(member[...], turned(product, turn[...], waves)).astype(BF16)


def table_kernel(waves, z0, z1, z2, z3, out, held):
    place = here()
    lines = z0.shape[0]
    span = held.shape[1]
    pieces = (z0.shape[1] - 2 * waves) // span
    for j, part in enumerate((z0, z1, z2, z3)):
        for i in range(pieces):
            at = pl.multiple_of(((place[2] ^ j) * pieces + i) * lines, lines)
            held[pl.ds(at, lines), :] = part[:, pl.ds(2 * waves + i * span, span)].astype(F32)
    out[...] = held[...].T.astype(BF16)


def near_kernel(starts, emit, neighbours, live, *refs):
    place = here()
    mine, theirs = refs[:5], refs[5 : 5 + (1 if starts[1] is not None else 2)]
    refs = refs[5 + len(theirs) :]
    blocks = refs[0]
    out_mine, out_theirs = refs[1], refs[2]
    image = refs[3] if emit else None
    held = refs[4]
    if not emit:
        source_blocks, blocks, arrived = blocks, refs[3], refs[5]
        copies = [
            pltpu.make_async_copy(source_blocks.at[n], blocks.at[n], arrived.at[n])
            for n in range(blocks.shape[0])
        ]
        for copy in copies:
            copy.start()
    spheres = out_mine.shape[0] // 2
    slots = blocks.shape[1]
    coeffs = blocks.shape[3]
    for j in range(5):
        for side in range(2):
            for r in range(2):
                rows = pl.ds(r * spheres, spheres)
                if starts[1] is not None:
                    value = mine[j][rows, pl.ds(starts[side], 2 * coeffs)]
                    if j == 4:
                        other = theirs[0][rows, pl.ds(starts[1 - side], 2 * coeffs)]
                        value = jnp.where(place[0] == 0, other, value)
                elif side == 0:
                    value = mine[j][rows, pl.ds(0, 2 * coeffs)]
                else:
                    value = theirs[j // 4][pl.ds((2 * (j % 4) + r) * spheres, spheres), :]
                value = value.astype(F32)
                at = pl.ds(j * spheres, spheres)
                held[at, side * 2 + r, :] = value[:, :coeffs]
                held[at, 4 + side * 2 + r, :] = value[:, coeffs:]
    if emit:
        first = place[0] == 0
        for r in range(2):
            own = mine[0][pl.ds(r * spheres, spheres), :].astype(F32)
            other = theirs[0][pl.ds(r * spheres, spheres), :].astype(F32)
            image[:, r, :] = jnp.where(first, own, other).astype(BF16)
            image[:, 2 + r, :] = jnp.where(first, other, own).astype(BF16)

    for n in range(spheres):
        real = jnp.zeros((8, coeffs), F32)
        imag = jnp.zeros((8, coeffs), F32)
        if not emit:
            copies[n].wait()
        for k in range(slots):
            source = neighbours[n, k]
            chip = source // spheres
            near = jnp.where(chip // 4 == place[3] // 4, chip ^ place[3], 4)
            value = held[near * spheres + source % spheres]
            alive = place[0] * slots + k < live[n]
            value = jnp.where(alive, value, 0.0).astype(BF16)
            real += jnp.dot(value, blocks[n, k, 0], preferred_element_type=F32)
            imag += jnp.dot(value, blocks[n, k, 1], preferred_element_type=F32)
        near_re = real[:4] - imag[4:]
        near_im = imag[:4] + real[4:]
        for r in range(2):
            row = pl.ds(r * spheres + n, 1)
            out_mine[row, pl.ds(0, coeffs)] = near_re[r : r + 1]
            out_mine[row, pl.ds(coeffs, coeffs)] = near_im[r : r + 1]
            out_theirs[row, pl.ds(0, coeffs)] = near_re[2 + r : 3 + r]
            out_theirs[row, pl.ds(coeffs, coeffs)] = near_im[2 + r : 3 + r]


def near_call(starts, emit, neighbours, live, mine, theirs, blocks):
    spheres, slots, _, coeffs, _ = blocks.shape
    rows = 2 * spheres
    outs = [jax.ShapeDtypeStruct((rows, 2 * coeffs), F32)] * 2
    if emit:
        outs.append(jax.ShapeDtypeStruct((spheres, 4, 2 * coeffs), BF16))
    else:
        outs.append(pltpu.VMEM(blocks.shape, BF16))
    full = [VM] * (len(mine) + len(theirs))
    return pl.pallas_call(
        functools.partial(near_kernel, starts, emit),
        out_shape=tuple(outs),
        in_specs=[SM] * 2 + full + [VM if emit else HB],
        out_specs=(VM,) * len(outs),
        scratch_shapes=[pltpu.VMEM((5 * spheres, 8, coeffs), F32)]
        + ([] if emit else [pltpu.SemaphoreType.DMA((spheres,))]),
        cost_estimate=pl.CostEstimate(
            flops=2 * 8 * 2 * coeffs * coeffs * spheres * slots,
            bytes_accessed=blocks.size * 2,
            transcendentals=0,
        ),
        compiler_params=pltpu.CompilerParams(vmem_limit_bytes=(4 if emit else 34) << 20),
    )(neighbours, live, *mine, *theirs, blocks)


def far_kernel(
    box, list_mine, list_theirs, z0, z1, z2, z3, table_mine, table_theirs, turn, dis, out,
    source, factor, field, local
):
    place = here()
    own_boxes, listed = list_mine.shape
    boxes = 2 * own_boxes
    waves = source.shape[2]
    spheres = local.shape[1]
    first = place[0] == 0
    total = jnp.zeros((2 * boxes, 2 * waves), F32)
    for part in (z0, z1, z2, z3):
        total += part[:, pl.ds(0, 2 * waves)].astype(F32)
    for r in range(2):
        re = total[r * boxes : (r + 1) * boxes, :waves]
        im = total[r * boxes : (r + 1) * boxes, waves:]
        source[:, r, :] = re
        source[:, 2 + r, :] = im
        source[:, 4 + r, :] = -im
        source[:, 6 + r, :] = re
    size = table_mine.shape[0]
    mine, theirs = table_mine[...].astype(F32), table_theirs[...].astype(F32)
    factor[pl.ds(0, size), :] = jnp.where(first, mine, theirs)
    factor[pl.ds(size, size), :] = jnp.where(first, theirs, mine)
    upper = lax.broadcasted_iota(jnp.int32, (8, waves), 0) < 4

    def one_box(b, carry):
        row = b % own_boxes
        is_mine = b // own_boxes == place[0]
        sums = [jnp.zeros((8, waves), F32) for _ in range(2)]
        for f in range(listed):
            which = jnp.where(is_mine, list_mine[row, f], list_theirs[row, f])
            at = (b * listed + f) * 2
            weight = jnp.where(upper, factor[pl.ds(at, 1), :], factor[pl.ds(at + 1, 1), :])
            sums[f % 2] = sums[f % 2] + weight * source[which]
        both = sums[0] + sums[1]
        field[b] = both[:4] + both[4:]
        return carry

    lax.fori_loop(box[0], box[spheres - 1] + 1, one_box, 0)
    for n in range(spheres):
        local[:, n, :] = field[box[n]]
    re = local[pl.ds(0, 2)].reshape(2 * spheres, waves)
    im = local[pl.ds(2, 2)].reshape(2 * spheres, waves)
    cosine = turn[pl.ds(0, 2 * spheres), pl.ds(0, waves)]
    sine = turn[pl.ds(0, 2 * spheres), pl.ds(waves, waves)]
    shifted = jnp.concatenate([re * cosine + im * sine, im * cosine - re * sine], axis=1)
    dims = (((1,), (1,)), ((), ()))
    out[...] = lax.dot_general(shifted.astype(BF16), dis[...], dims, preferred_element_type=F32)


def scatter_kernel(far, near_mine, near_got, tmatrix, current, out):
    coeffs = tmatrix.shape[2]
    total = far[...] + (near_mine[...] + near_got[...])
    t_re = jnp.concatenate([tmatrix[:, 0], tmatrix[:, 0]], axis=0)
    t_im = jnp.concatenate([tmatrix[:, 1], tmatrix[:, 1]], axis=0)
    f_re, f_im = total[:, :coeffs], total[:, coeffs:]
    start = current[:, pl.ds(0, 2 * coeffs)].astype(F32)
    out[:, pl.ds(0, coeffs)] = (start[:, :coeffs] - (t_re * f_re - t_im * f_im)).astype(BF16)
    out[:, pl.ds(coeffs, coeffs)] = (start[:, coeffs:] - (t_re * f_im + t_im * f_re)).astype(BF16)


def join_kernel(mine, theirs, out):
    spheres = out.shape[0]
    first = lax.axis_index("far") == 0
    for r in range(2):
        own = mine[pl.ds(r * spheres, spheres), :].astype(F32)
        other = theirs[pl.ds(r * spheres, spheres), :].astype(F32)
        out[:, r, :] = jnp.where(first, own, other).astype(BF16)
        out[:, 2 + r, :] = jnp.where(first, other, own).astype(BF16)


def swap_far(block):
    return lax.ppermute(block, "far", [(0, 1), (1, 0)])


def kernel_shards(
    vectors, near_blocks, neighbours, live_counts, tmatrix, agg_matrix, sphere_box, agg_angle,
    far_list, far_factors, dis_matrix
):
    spheres, newton, width = vectors.shape
    own_boxes, listed = far_list.shape
    boxes = 2 * own_boxes
    waves = agg_matrix.shape[1] // 2
    rows = spheres * newton // 2
    entries = own_boxes * listed * 2
    later = (near_blocks, agg_matrix, neighbours, live_counts)
    message = call(
        pack_kernel,
        [((rows, 1024 + waves + entries), BF16)],
        [SM, VM, VM, VM] + [HB] * 4,
        (sphere_box, vectors, agg_angle, far_factors.reshape(entries, -1), *later),
        limit=60 << 20,
        held=True,
    )[0]
    list_theirs = swap_far(far_list)
    current = message
    table = None
    for step in range(2):
        if step == 0:
            parts = xor_gather(message, (1, 2, 3))
            parts, list_theirs = lax.optimization_barrier((parts, list_theirs))
            block, turn, member, _ = call(
                functools.partial(first_waves_kernel, boxes),
                [
                    ((2 * boxes, 2 * waves + waves // 4 * entries // (2 * boxes)), BF16),
                    ((4 * rows, 2 * waves), F32),
                    ((4 * rows, 2 * boxes), BF16),
                    ((waves // 4, entries), F32),
                ],
                [VM] * 5,
                (*parts, agg_matrix),
            )
        else:
            parts = xor_gather(current, (1, 2, 3))
            block, around = call(
                next_waves_kernel,
                [((2 * boxes, 2 * waves), BF16), ((4 * rows, width), BF16)],
                [VM] * 7,
                (*parts, agg_matrix, turn, member),
            )
        edge = edge_from_plane(parts[3]) if step else edge_of_second_core(parts[3])
        pieces = [block]
        for mask in (4, 8, 12):
            pieces.append(swap_near(block, mask))
        mine = (*parts, edge)
        if step == 0:
            passed = edge_to_first_core(edge)
            near_mine, near_theirs, held_blocks = near_call(
                (0, 512), False, neighbours, live_counts, mine, (passed,), near_blocks
            )
        else:
            around = swap_far(around)
            theirs = (around, swap_far(edge))
            near_mine, near_theirs, first_image = near_call(
                (0, None), True, neighbours, live_counts, mine, theirs, held_blocks
            )
        near_got = swap_far(near_theirs)
        if step == 0:
            pieces, near_mine = lax.optimization_barrier((pieces, near_mine))
            table = call(
                functools.partial(table_kernel, waves),
                [((entries, waves), BF16)],
                [VM] * 4,
                (*pieces,),
                [pltpu.VMEM((waves, entries), F32)],
            )[0]
            table = (table, swap_far(table))
        far_field = call(
            far_kernel,
            [((rows, width), F32)],
            [SM] * 3 + [VM] * 8,
            (
                sphere_box, far_list, list_theirs, *pieces, *table, turn, dis_matrix.T
            ),
            [
                pltpu.VMEM((boxes, 8, waves), F32),
                pltpu.VMEM((2 * entries, waves), F32),
                pltpu.VMEM((boxes, 4, waves), F32),
                pltpu.VMEM((4, spheres, waves), F32),
            ],
        )[0]
        current = call(
            scatter_kernel,
            [((rows, width), BF16)],
            [VM] * 5,
            (far_field, near_mine, near_got, tmatrix, current),
        )[0]
    second_image = call(
        join_kernel,
        [((spheres, newton, width), BF16)],
        [VM, VM],
        (current, swap_far(current)),
    )[0]
    return first_image, second_image


def shards(*args):
    if lax.axis_size("near") == 16 and lax.axis_size("far") == 2:
        return kernel_shards(*args)
    return plain_shards(*args)


def solution(mesh):
    return jax.shard_map(
        shards,
        mesh=mesh,
        in_specs=(
            P("near", None, None),
            P("near", "far", None, None, None),
            P("near", "far"),
            P("near"),
            P("near", None, None),
            P(),
            P("near"),
            P("near", None),
            P("far", None),
            P("far", None, None, "near"),
            P(),
        ),
        out_specs=(P("near", None, None), P("near", None, None)),
        check_vma=False,
    )
```

```python
import functools

import jax
import jax.numpy as jnp
from jax import lax
from jax.experimental import pallas as pl
from jax.experimental.pallas import tpu as pltpu
from jax.sharding import PartitionSpec as P

F32 = jnp.float32
BF16 = jnp.bfloat16
RADIX = 4


def complex_mul(left_re, left_im, right_re, right_im):
    return (left_re * right_re - left_im * right_im, left_re * right_im + left_im * right_re)


def swap_near(block, mask):
    count = lax.axis_size("near")
    return lax.ppermute(block, "near", [(i, i ^ mask) for i in range(count)])


def phase_masks():
    count = lax.axis_size("near")
    phases, step = [], 1
    while step < count:
        radix = min(RADIX, count // step)
        phases.append([step * j for j in range(1, radix)])
        step *= radix
    return phases


def xor_gather(block, masks):
    return [block] + [swap_near(block, mask) for mask in masks]


def in_order(parts, masks):
    step = masks[0]
    digit = lax.axis_index("near") // step % len(parts)
    stacked = jnp.stack(parts)
    return jnp.take(stacked, jnp.arange(len(parts)) ^ digit, axis=0)


def edge_rows(block):
    count = lax.axis_size("near")
    pairs = []
    for low in range(RADIX, count, RADIX):
        pairs.append((low - 1, low))
        pairs.append((low, low - 1))
    return lax.ppermute(block, "near", pairs) if pairs else jnp.zeros_like(block)


def edge_from_plane(diagonal):
    count = lax.axis_size("near")
    up = [(i, i + RADIX) for i in range(0, count - RADIX, RADIX)]
    down = [(i + RADIX, i) for i in range(RADIX - 1, count - RADIX, RADIX)]
    return lax.ppermute(diagonal, "near", up + down)


def over_far(block):
    count = lax.axis_size("far")
    if count == 2:
        other = lax.ppermute(block, "far", [(0, 1), (1, 0)])
        first = lax.axis_index("far") == 0
        return jnp.stack([jnp.where(first, block, other), jnp.where(first, other, block)])
    return lax.all_gather(block, "far", axis=0)


def near_share(partial, share):
    count = lax.axis_size("far")
    far_pos = lax.axis_index("far")
    mine = lax.dynamic_slice_in_dim(partial, far_pos % (partial.shape[1] // share) * share, share, 1)
    if count == 2:
        theirs = lax.dynamic_slice_in_dim(partial, (1 - far_pos) * share, share, 1)
        return mine + lax.ppermute(theirs, "far", [(0, 1), (1, 0)])
    total = lax.psum(partial, "far")
    return lax.dynamic_slice_in_dim(total, far_pos % (partial.shape[1] // share) * share, share, 1)


def plain_shards(
    vectors,
    near_blocks,
    neighbours,
    live_counts,
    tmatrix,
    agg_matrix,
    sphere_box,
    agg_angle,
    far_list,
    far_factors,
    dis_matrix,
):
    spheres, newton, width = vectors.shape
    coeffs = width // 2
    slots = neighbours.shape[1]
    far_count = lax.axis_size("far")
    own_boxes, listed = far_list.shape
    boxes = own_boxes * far_count
    waves = agg_matrix.shape[1] // 2
    share = newton // min(far_count, newton)
    splits = newton // share
    near_pos = lax.axis_index("near")
    far_pos = lax.axis_index("far")
    phases = phase_masks()
    rows = spheres * share

    def own_share(block):
        return lax.dynamic_slice_in_dim(block, far_pos % splits * share, share, 1)

    rounded = lax.reduce_precision(agg_angle, 8, 7)
    hi, low = rounded.astype(BF16), (agg_angle - rounded).astype(BF16)
    factors = far_factors.astype(BF16).reshape(-1, far_factors.shape[-1]).T
    lists = over_far_lists(far_list)
    extra = jnp.concatenate(
        [
            jnp.repeat(sphere_box, share).astype(BF16)[:, None],
            jnp.stack([hi, low]).reshape(rows, -1),
            factors.reshape(rows, -1),
        ],
        axis=1,
    )
    angle_width = 2 * spheres * waves // rows

    cosine = jnp.cos(agg_angle)
    sine = jnp.sin(agg_angle)
    alive = (far_pos * slots + jnp.arange(slots, dtype=jnp.int32))[None, :] < live_counts[:, None]
    chip = neighbours // spheres
    place = jnp.where(chip // RADIX == near_pos // RADIX, chip ^ near_pos, RADIX)
    local_index = place * spheres + neighbours % spheres

    state = {}
    images = []
    current = own_share(vectors)
    for step in range(2):
        flat = current.reshape(rows, width)
        edge = edge_rows(current)
        message = jnp.concatenate([flat, extra], axis=1) if step == 0 else flat
        parts = xor_gather(message, phases[0])
        group = len(parts)
        around = [p[:, :width].reshape(spheres, share, width) for p in parts]
        full = over_far(jnp.stack(around + [edge]))[:splits]
        full = jnp.moveaxis(full, 0, 2).reshape((group + 1) * spheres, newton, width)
        if step == 1:
            images.append(full[:spheres])
        if step == 0:
            box_ids = jnp.concatenate([p[:, width].reshape(spheres, share)[:, 0] for p in parts])
            angles = jnp.stack(
                [
                    p[:, width + 1 : width + 1 + angle_width].reshape(2, spheres, waves)
                    for p in parts
                ]
            ).astype(F32)
            angles = (angles[:, 0] + angles[:, 1]).reshape(group * spheres, waves)
            state["cos"], state["sin"] = jnp.cos(angles), jnp.sin(angles)
            state["member"] = (
                box_ids.astype(jnp.int32)[None, :] == jnp.arange(boxes, dtype=jnp.int32)[:, None]
            ).astype(F32)
            table = in_order([p[:, width + 1 + angle_width :] for p in parts], phases[0])
        product = jnp.dot(
            jnp.concatenate(around).reshape(group * rows, width),
            agg_matrix,
            preferred_element_type=F32,
        ).reshape(group * spheres, share, 2, waves)
        out_re, out_im = complex_mul(
            product[:, :, 0], product[:, :, 1], state["cos"][:, None], state["sin"][:, None]
        )
        stacked = jnp.concatenate([out_re, out_im], axis=-1)
        sums = jnp.einsum("bn,nrq->brq", state["member"], stacked, precision=lax.Precision.HIGHEST)
        for masks in phases[1:]:
            block = sums.astype(BF16).reshape(boxes * share, 2 * waves)
            if step == 0:
                block = jnp.concatenate([block, table.reshape(boxes * share, -1)], axis=1)
            pieces = xor_gather(block, masks)
            sums = sum(p[:, : 2 * waves].astype(F32) for p in pieces)
            sums = sums.reshape(boxes, share, 2 * waves)
            if step == 0:
                table = in_order([p[:, 2 * waves :] for p in pieces], masks)
        if step == 0:
            table = over_far(table.reshape(waves, own_boxes, listed, 2))
            table = table.transpose(0, 2, 3, 4, 1).reshape(boxes, listed, 2, waves)
            state["factors"] = table[sphere_box].astype(F32)
            state["sources"] = (
                lists[sphere_box][:, :, None] == jnp.arange(boxes, dtype=jnp.int32)
            ).astype(F32)
        gathered = jnp.where(alive[:, :, None, None], full[local_index], jnp.zeros((), BF16))
        both = jnp.concatenate([gathered[..., :coeffs], gathered[..., coeffs:]], axis=2)
        with_real = jnp.einsum(
            "nkrc,nkcd->nrd", both, near_blocks[:, :, 0], preferred_element_type=F32
        )
        with_imag = jnp.einsum(
            "nkrc,nkcd->nrd", both, near_blocks[:, :, 1], preferred_element_type=F32
        )
        near_re = with_real[:, :newton] - with_imag[:, newton:]
        near_im = with_imag[:, :newton] + with_real[:, newton:]
        near_field = near_share(jnp.concatenate([near_re, near_im], axis=-1), share)
        picked = jnp.einsum(
            "nfb,brq->nfrq", state["sources"], sums, precision=lax.Precision.HIGHEST
        )
        fac = state["factors"]
        in_re, in_im = complex_mul(
            fac[:, :, None, 0], fac[:, :, None, 1], picked[..., :waves], picked[..., waves:]
        )
        in_re, in_im = jnp.sum(in_re, axis=1), jnp.sum(in_im, axis=1)
        local_re, local_im = complex_mul(in_re, in_im, cosine[:, None], -sine[:, None])
        local_waves = jnp.concatenate([local_re, local_im], axis=-1).astype(BF16)
        far_field = jnp.dot(
            local_waves.reshape(rows, 2 * waves), dis_matrix, preferred_element_type=F32
        ).reshape(spheres, share, width)
        field = near_field + far_field
        scat_re, scat_im = complex_mul(
            tmatrix[:, None, 0], tmatrix[:, None, 1], field[..., :coeffs], field[..., coeffs:]
        )
        current = (current.astype(F32) - jnp.concatenate([scat_re, scat_im], axis=-1)).astype(BF16)
    last = over_far(current)[:splits]
    images.append(jnp.moveaxis(last, 0, 1).reshape(spheres, newton, width))
    return tuple(images)


def over_far_lists(far_list):
    gathered = over_far(far_list)
    return gathered.reshape(-1, far_list.shape[1])


VM = pl.BlockSpec(memory_space=pltpu.VMEM)
SM = pl.BlockSpec(memory_space=pltpu.SMEM)
HB = pl.BlockSpec(memory_space=pl.ANY)


def call(kernel, outs, specs, args, scratch=(), flops=0, moved=6 << 20, limit=4 << 20, held=False):
    make = pltpu.VMEM if held else jax.ShapeDtypeStruct
    return pl.pallas_call(
        kernel,
        out_shape=tuple(make(shape, kind) for shape, kind in outs),
        in_specs=list(specs),
        out_specs=(VM,) * len(outs),
        scratch_shapes=list(scratch),
        cost_estimate=pl.CostEstimate(flops=flops, bytes_accessed=moved, transcendentals=0),
        compiler_params=pltpu.CompilerParams(vmem_limit_bytes=limit),
    )(*args)


def here():
    near_pos = lax.axis_index("near")
    return lax.axis_index("far"), near_pos % 4, near_pos // 4, near_pos


def pack_kernel(box, vectors, angle, factors, *refs):
    out, first_block, arrived = refs[-3:]
    copy = pltpu.make_async_copy(refs[0].at[pl.ds(0, 1)], first_block, arrived)
    copy.start()
    place = here()
    spheres, newton, width = vectors.shape
    share = newton // 2
    waves = angle.shape[1]
    first = place[0] == 0
    values = vectors[...].astype(F32)
    for r in range(share):
        low, high = values[:, r], values[:, share + r]
        rows = pl.ds(r * spheres, spheres)
        out[rows, pl.ds(0, width)] = jnp.where(first, low, high).astype(BF16)
        out[rows, pl.ds(512, width)] = jnp.where(first, high, low).astype(BF16)
    lane = lax.broadcasted_iota(jnp.int32, (spheres * share, 512 - width), 0) % spheres
    ids = jnp.zeros((spheres * share, 512 - width), F32)
    for n in range(spheres):
        ids = jnp.where(lane == n, box[n].astype(F32), ids)
    out[:, pl.ds(width, 512 - width)] = ids.astype(BF16)
    hi = angle[...].astype(BF16)
    low = (angle[...] - hi.astype(F32)).astype(BF16)
    out[pl.ds(0, spheres), pl.ds(1024, waves)] = hi
    out[pl.ds(spheres, spheres), pl.ds(1024, waves)] = low
    out[:, pl.ds(1024 + waves, factors.shape[0])] = factors[...].T.astype(BF16)
    copy.wait()


def sum_rows(member, waves):
    dims = (((0,), (0,)), ((), ()))
    hi = waves.astype(BF16)
    low = (waves - hi.astype(F32)).astype(BF16)
    return lax.dot_general(member, hi, dims, preferred_element_type=F32) + lax.dot_general(
        member, low, dims, preferred_element_type=F32
    )


def turned(product, turn, waves):
    cosine, sine = turn[:, :waves], turn[:, waves:]
    re, im = product[:, :waves], product[:, waves:]
    return jnp.concatenate([re * cosine - im * sine, re * sine + im * cosine], axis=1)


def first_waves_kernel(boxes, p0, p1, p2, p3, agg, out, turn, member, table):
    place = here()
    parts = (p0, p1, p2, p3)
    width = agg.shape[0]
    waves = agg.shape[1] // 2
    rows = p0.shape[0]
    half = rows // 2
    held = table.shape[0] // 4
    for j, part in enumerate(parts):
        angle = part[pl.ds(0, half), pl.ds(1024, waves)].astype(F32)
        angle += part[pl.ds(half, half), pl.ds(1024, waves)].astype(F32)
        both = jnp.concatenate([jnp.cos(angle), jnp.sin(angle)], axis=1)
        turn[pl.ds(j * rows, half), :] = both
        turn[pl.ds(j * rows + half, half), :] = both
        ids = part[:, pl.ds(width, 1)].astype(F32)
        row = lax.broadcasted_iota(jnp.int32, (rows, 2 * boxes), 0) // half
        col = lax.broadcasted_iota(jnp.int32, (rows, 2 * boxes), 1)
        hit = (ids == (col % boxes).astype(F32)) & (row == col // boxes)
        member[pl.ds(j * rows, rows), :] = jnp.where(hit, 1.0, 0.0).astype(BF16)
        at = pl.multiple_of((place[1] ^ j) * held, held)
        table[pl.ds(at, held), :] = part[:, pl.ds(1024 + waves, table.shape[1])].astype(F32)
    flat = jnp.concatenate([p[:, pl.ds(0, width)] for p in parts], axis=0)
    product = jnp.dot(flat, agg[...], preferred_element_type=F32)
    sums = sum_rows(member[...], turned(product, turn[...], waves))
    out[:, pl.ds(0, 2 * waves)] = sums.astype(BF16)
    lines = out.shape[0]
    span = table.shape[1]
    for j in range(table.shape[0] // lines):
        out[:, pl.ds(2 * waves + j * span, span)] = table[pl.ds(j * lines, lines), :].astype(BF16)


def next_waves_kernel(p0, p1, p2, p3, agg, turn, member, out, around):
    waves = agg.shape[1] // 2
    rows = p0.shape[0]
    for j, part in enumerate((p0, p1, p2, p3)):
        around[pl.ds(j * rows, rows), :] = part[...]
    flat = jnp.concatenate([p0[...], p1[...], p2[...], p3[...]], axis=0)
    product = jnp.dot(flat, agg[...], preferred_element_type=F32)
    out[...] = sum_rows(member[...], turned(product, turn[...], waves)).astype(BF16)


def table_kernel(waves, z0, z1, z2, z3, out, held):
    place = here()
    lines = z0.shape[0]
    span = held.shape[1]
    pieces = (z0.shape[1] - 2 * waves) // span
    for j, part in enumerate((z0, z1, z2, z3)):
        for i in range(pieces):
            at = pl.multiple_of(((place[2] ^ j) * pieces + i) * lines, lines)
            held[pl.ds(at, lines), :] = part[:, pl.ds(2 * waves + i * span, span)].astype(F32)
    out[...] = held[...].T.astype(BF16)


def near_kernel(starts, emit, neighbours, live, *refs):
    place = here()
    mine, theirs = refs[:5], refs[5 : 5 + (5 if starts[1] is not None else 2)]
    refs = refs[5 + len(theirs) :]
    first_block, blocks = refs[:2]
    out_mine, out_theirs = refs[2], refs[3]
    image = refs[4] if emit else None
    held = refs[5]
    if not emit:
        source_blocks, blocks, arrived = blocks, refs[4], refs[6]
        copies = [
            pltpu.make_async_copy(source_blocks.at[n + 1], blocks.at[n], arrived.at[n])
            for n in range(blocks.shape[0])
        ]
        for copy in copies:
            copy.start()
    spheres = out_mine.shape[0] // 2
    slots = blocks.shape[1]
    coeffs = blocks.shape[3]
    for j in range(5):
        for side in range(2):
            for r in range(2):
                rows = pl.ds(r * spheres, spheres)
                if side == 0:
                    value = mine[j][rows, pl.ds(0, 2 * coeffs)]
                elif starts[1] is not None:
                    value = theirs[j][rows, pl.ds(starts[1], 2 * coeffs)]
                else:
                    value = theirs[j // 4][pl.ds((2 * (j % 4) + r) * spheres, spheres), :]
                value = value.astype(F32)
                at = pl.ds(j * spheres, spheres)
                held[at, side * 2 + r, :] = value[:, :coeffs]
                held[at, 4 + side * 2 + r, :] = value[:, coeffs:]
    if emit:
        first = place[0] == 0
        for r in range(2):
            own = mine[0][pl.ds(r * spheres, spheres), :].astype(F32)
            other = theirs[0][pl.ds(r * spheres, spheres), :].astype(F32)
            image[:, r, :] = jnp.where(first, own, other).astype(BF16)
            image[:, 2 + r, :] = jnp.where(first, other, own).astype(BF16)

    for n in range(spheres):
        real = jnp.zeros((8, coeffs), F32)
        imag = jnp.zeros((8, coeffs), F32)
        block = blocks.at[n - 1] if n else first_block.at[0]
        if n and not emit:
            copies[n - 1].wait()
        for k in range(slots):
            source = neighbours[n, k]
            chip = source // spheres
            near = jnp.where(chip // 4 == place[3] // 4, chip ^ place[3], 4)
            value = held[near * spheres + source % spheres]
            alive = place[0] * slots + k < live[n]
            value = jnp.where(alive, value, 0.0).astype(BF16)
            real += jnp.dot(value, block[k, 0], preferred_element_type=F32)
            imag += jnp.dot(value, block[k, 1], preferred_element_type=F32)
        near_re = real[:4] - imag[4:]
        near_im = imag[:4] + real[4:]
        for r in range(2):
            row = pl.ds(r * spheres + n, 1)
            out_mine[row, pl.ds(0, coeffs)] = near_re[r : r + 1]
            out_mine[row, pl.ds(coeffs, coeffs)] = near_im[r : r + 1]
            out_theirs[row, pl.ds(0, coeffs)] = near_re[2 + r : 3 + r]
            out_theirs[row, pl.ds(coeffs, coeffs)] = near_im[2 + r : 3 + r]


def near_call(starts, emit, neighbours, live, mine, theirs, first_block, blocks):
    slots, _, coeffs, _ = blocks.shape[1:]
    spheres = live.shape[0]
    rows = 2 * spheres
    outs = [jax.ShapeDtypeStruct((rows, 2 * coeffs), F32)] * 2
    if emit:
        outs.append(jax.ShapeDtypeStruct((spheres, 4, 2 * coeffs), BF16))
    else:
        outs.append(pltpu.VMEM((spheres - 1,) + blocks.shape[1:], BF16))
    full = [VM] * (len(mine) + len(theirs))
    return pl.pallas_call(
        functools.partial(near_kernel, starts, emit),
        out_shape=tuple(outs),
        in_specs=[SM] * 2 + full + [VM, VM if emit else HB],
        out_specs=(VM,) * len(outs),
        scratch_shapes=[pltpu.VMEM((5 * spheres, 8, coeffs), F32)]
        + ([] if emit else [pltpu.SemaphoreType.DMA((spheres - 1,))]),
        cost_estimate=pl.CostEstimate(
            flops=2 * 8 * 2 * coeffs * coeffs * spheres * slots,
            bytes_accessed=blocks.size * 2,
            transcendentals=0,
        ),
        compiler_params=pltpu.CompilerParams(vmem_limit_bytes=(4 if emit else 34) << 20),
    )(neighbours, live, *mine, *theirs, first_block, blocks)


def far_kernel(
    box, list_mine, list_theirs, z0, z1, z2, z3, table_mine, table_theirs, turn, dis, out,
    source, factor, field, local
):
    place = here()
    own_boxes, listed = list_mine.shape
    boxes = 2 * own_boxes
    waves = source.shape[2]
    spheres = local.shape[1]
    first = place[0] == 0
    total = jnp.zeros((2 * boxes, 2 * waves), F32)
    for part in (z0, z1, z2, z3):
        total += part[:, pl.ds(0, 2 * waves)].astype(F32)
    for r in range(2):
        re = total[r * boxes : (r + 1) * boxes, :waves]
        im = total[r * boxes : (r + 1) * boxes, waves:]
        source[:, r, :] = re
        source[:, 2 + r, :] = im
        source[:, 4 + r, :] = -im
        source[:, 6 + r, :] = re
    size = table_mine.shape[0]
    mine, theirs = table_mine[...].astype(F32), table_theirs[...].astype(F32)
    factor[pl.ds(0, size), :] = jnp.where(first, mine, theirs)
    factor[pl.ds(size, size), :] = jnp.where(first, theirs, mine)
    upper = lax.broadcasted_iota(jnp.int32, (8, waves), 0) < 4

    def one_box(b, carry):
        row = b % own_boxes
        is_mine = b // own_boxes == place[0]
        sums = [jnp.zeros((8, waves), F32) for _ in range(2)]
        for f in range(listed):
            which = jnp.where(is_mine, list_mine[row, f], list_theirs[row, f])
            at = (b * listed + f) * 2
            weight = jnp.where(upper, factor[pl.ds(at, 1), :], factor[pl.ds(at + 1, 1), :])
            sums[f % 2] = sums[f % 2] + weight * source[which]
        both = sums[0] + sums[1]
        field[b] = both[:4] + both[4:]
        return carry

    lax.fori_loop(box[0], box[spheres - 1] + 1, one_box, 0)
    for n in range(spheres):
        local[:, n, :] = field[box[n]]
    re = local[pl.ds(0, 2)].reshape(2 * spheres, waves)
    im = local[pl.ds(2, 2)].reshape(2 * spheres, waves)
    cosine = turn[pl.ds(0, 2 * spheres), pl.ds(0, waves)]
    sine = turn[pl.ds(0, 2 * spheres), pl.ds(waves, waves)]
    shifted = jnp.concatenate([re * cosine + im * sine, im * cosine - re * sine], axis=1)
    dims = (((1,), (1,)), ((), ()))
    out[...] = lax.dot_general(shifted.astype(BF16), dis[...], dims, preferred_element_type=F32)


def scatter_kernel(far, near_mine, near_got, tmatrix, current, out):
    coeffs = tmatrix.shape[2]
    total = far[...] + (near_mine[...] + near_got[...])
    t_re = jnp.concatenate([tmatrix[:, 0], tmatrix[:, 0]], axis=0)
    t_im = jnp.concatenate([tmatrix[:, 1], tmatrix[:, 1]], axis=0)
    f_re, f_im = total[:, :coeffs], total[:, coeffs:]
    start = current[:, pl.ds(0, 2 * coeffs)].astype(F32)
    out[:, pl.ds(0, coeffs)] = (start[:, :coeffs] - (t_re * f_re - t_im * f_im)).astype(BF16)
    out[:, pl.ds(coeffs, coeffs)] = (start[:, coeffs:] - (t_re * f_im + t_im * f_re)).astype(BF16)


def join_kernel(mine, theirs, out):
    spheres = out.shape[0]
    first = lax.axis_index("far") == 0
    for r in range(2):
        own = mine[pl.ds(r * spheres, spheres), :].astype(F32)
        other = theirs[pl.ds(r * spheres, spheres), :].astype(F32)
        out[:, r, :] = jnp.where(first, own, other).astype(BF16)
        out[:, 2 + r, :] = jnp.where(first, other, own).astype(BF16)


def swap_far(block):
    return lax.ppermute(block, "far", [(0, 1), (1, 0)])


def kernel_shards(
    vectors, near_blocks, neighbours, live_counts, tmatrix, agg_matrix, sphere_box, agg_angle,
    far_list, far_factors, dis_matrix
):
    spheres, newton, width = vectors.shape
    own_boxes, listed = far_list.shape
    boxes = 2 * own_boxes
    waves = agg_matrix.shape[1] // 2
    rows = spheres * newton // 2
    entries = own_boxes * listed * 2
    later = (near_blocks, agg_matrix, neighbours, live_counts)
    message, first_block = call(
        pack_kernel,
        [((rows, 1024 + waves + entries), BF16), ((1,) + near_blocks.shape[1:], BF16)],
        [SM, VM, VM, VM] + [HB] * 4,
        (sphere_box, vectors, agg_angle, far_factors.reshape(entries, -1), *later),
        [pltpu.SemaphoreType.DMA],
        limit=56 << 20,
        held=True,
    )
    list_theirs = swap_far(far_list)
    current = message
    table = None
    for step in range(2):
        if step == 0:
            parts = xor_gather(message, (1, 2, 3))
            parts, list_theirs = lax.optimization_barrier((parts, list_theirs))
            block, turn, member, _ = call(
                functools.partial(first_waves_kernel, boxes),
                [
                    ((2 * boxes, 2 * waves + waves // 4 * entries // (2 * boxes)), BF16),
                    ((4 * rows, 2 * waves), F32),
                    ((4 * rows, 2 * boxes), BF16),
                    ((waves // 4, entries), F32),
                ],
                [VM] * 5,
                (*parts, agg_matrix),
            )
        else:
            parts = xor_gather(current, (1, 2, 3))
            block, around = call(
                next_waves_kernel,
                [((2 * boxes, 2 * waves), BF16), ((4 * rows, width), BF16)],
                [VM] * 7,
                (*parts, agg_matrix, turn, member),
            )
        edge = edge_from_plane(parts[3])
        pieces = [block]
        for mask in (4, 8, 12):
            pieces.append(swap_near(block, mask))
        mine = (*parts, edge)
        if step == 0:
            near_mine, near_theirs, held_blocks = near_call(
                (0, 512), False, neighbours, live_counts, mine, mine, first_block, near_blocks
            )
        else:
            around = swap_far(around)
            theirs = (around, swap_far(edge))
            near_mine, near_theirs, first_image = near_call(
                (0, None), True, neighbours, live_counts, mine, theirs, first_block, held_blocks
            )
        near_got = swap_far(near_theirs)
        if step == 0:
            pieces, near_mine = lax.optimization_barrier((pieces, near_mine))
            table = call(
                functools.partial(table_kernel, waves),
                [((entries, waves), BF16)],
                [VM] * 4,
                (*pieces,),
                [pltpu.VMEM((waves, entries), F32)],
            )[0]
            table = (table, swap_far(table))
        far_field = call(
            far_kernel,
            [((rows, width), F32)],
            [SM] * 3 + [VM] * 8,
            (
                sphere_box, far_list, list_theirs, *pieces, *table, turn, dis_matrix.T
            ),
            [
                pltpu.VMEM((boxes, 8, waves), F32),
                pltpu.VMEM((2 * entries, waves), F32),
                pltpu.VMEM((boxes, 4, waves), F32),
                pltpu.VMEM((4, spheres, waves), F32),
            ],
        )[0]
        current = call(
            scatter_kernel,
            [((rows, width), BF16)],
            [VM] * 5,
            (far_field, near_mine, near_got, tmatrix, current),
        )[0]
    second_image = call(
        join_kernel,
        [((spheres, newton, width), BF16)],
        [VM, VM],
        (current, swap_far(current)),
    )[0]
    return first_image, second_image


def shards(*args):
    if lax.axis_size("near") == 16 and lax.axis_size("far") == 2:
        return kernel_shards(*args)
    return plain_shards(*args)


def solution(mesh):
    return jax.shard_map(
        shards,
        mesh=mesh,
        in_specs=(
            P("near", None, None),
            P("near", "far", None, None, None),
            P("near", "far"),
            P("near"),
            P("near", None, None),
            P(),
            P("near"),
            P("near", None),
            P("far", None),
            P("far", None, None, "near"),
            P(),
        ),
        out_specs=(P("near", None, None), P("near", None, None)),
        check_vma=False,
    )
```
